256 devices in a mesh: gx: 16 (over z, x_hi), gy: 16 (over y, x_lo, core).
Axes of the slice: x: 4 (x_hi: 2, x_lo: 2; x = x_hi * 2 + x_lo), y: 4, z: 8, core: 2. Of those that a mesh axis runs over, the one named last changes fastest.
Arguments:
- map_codes: int32 [4096, 4096], P('gy', 'gx'), may hold values from 0 to 63
- reward_table: float32 [4, 64], replicated, may hold values from -1 to 1
- start_cell: int32 [524288], P(('gx', 'gy')), may hold values from 0 to 65535, as said below
- agent_task: int32 [524288], P(('gx', 'gy')), may hold values from 0 to 3
- actions: int32 [16, 524288], P(None, ('gx', 'gy')), may hold values from 0 to 4, as said below
Outputs:
- values: float32 [4, 4096, 4096], P(None, 'gy', 'gx')
- agent_value: float32 [524288], P(('gx', 'gy'))
The draws below stay inside these ranges and needn't reach their ends.
Inputs may be any that keep to these rules, and one draw needn't show every extreme that they name: `start_cell`: each agent starts inside the tile of its block. `actions`: 0 stays, 1 and 2 move one row up and down, 3 and 4 one column left and right. After its moves every agent stands in its starting tile or in one of the eight tiles around it (diagonal ones included); at most 128 agents of one block stand in any one of those eight tiles, and for every block exactly 128 stand in one of them.
All inputs are finite; a program needn't handle non-finite values.
Results may differ from the reference program's by a relative error of at most 0.00026.
Values sent between devices are 32-bit elements; how exact they have to be, the bound alone decides.
A program may use at most 64 MiB of HBM per device.

```python
import jax
import jax.numpy as jnp
from jax import lax

CR = 256
CC = 256
TASKS = 4
AG_DEV = 2048
CAP = 128
STEPS = 16
SWEEPS = 16
CODES = 64
TERMINAL = 2
NR = 4096
NC = 4096
AGENTS = 524288
N_GY = 16


DIRECTION_ROWS = (-1, -1, -1, 0, 0, 1, 1, 1, 0)


DIRECTION_COLS = (-1, 0, 1, -1, 1, -1, 0, 1, 0)


def component(key_list, heading, crossing, extent, reach):
    layout = heading.shape
    inward = jax.random.randint(key_list[0], layout, 0, reach, dtype=jnp.int32)
    second = jax.random.randint(key_list[1], layout, 0, reach, dtype=jnp.int32)
    spread = jax.random.randint(key_list[2], layout, 0, 2 * reach + 1, dtype=jnp.int32)
    middle = jax.random.randint(key_list[3], layout, 0, extent - 4 * reach, dtype=jnp.int32)
    across = inward + 1 + second
    anchor_plus = extent - 1 - inward
    offset_plus = jnp.where(crossing, across, -reach + spread % (inward + reach + 1))
    anchor_minus = inward
    offset_minus = jnp.where(crossing, -across, reach - spread % (inward + reach + 1))
    anchor_zero = 2 * reach + middle
    offset_zero = -reach + spread
    anchor = jnp.where(heading > 0, anchor_plus, jnp.where(heading < 0, anchor_minus, anchor_zero))
    offset = jnp.where(heading > 0, offset_plus, jnp.where(heading < 0, offset_minus, offset_zero))
    return (anchor, offset)


def plan_agents(key):
    block_count = AGENTS // AG_DEV
    reach = STEPS // 4
    key_list = jax.random.split(jax.random.fold_in(key, 31), 16)
    scores = jax.random.randint(key_list[0], (block_count, AG_DEV), 0, (1 << 30) // AG_DEV, dtype=jnp.int32) * AG_DEV + jnp.arange(AG_DEV, dtype=jnp.int32)[None, :]
    roles = jnp.argsort(jnp.argsort(scores, axis=1), axis=1).astype(jnp.int32)
    direction = jnp.where(roles < 8 * CAP, roles // CAP, 8)
    favoured = jax.random.randint(key_list[1], (block_count, 1), 0, 8, dtype=jnp.int32)
    tossed = jax.random.randint(key_list[2], (block_count, AG_DEV), 0, 2, dtype=jnp.int32)
    crossing = (direction < 8) & ((direction == favoured) | (tossed == 1))
    row_heading = jnp.array(DIRECTION_ROWS, jnp.int32)[direction]
    col_heading = jnp.array(DIRECTION_COLS, jnp.int32)[direction]
    row_anchor, row_offset = component(key_list[3:7], row_heading, crossing, CR, reach)
    col_anchor, col_offset = component(key_list[7:11], col_heading, crossing, CC, reach)
    start_cell = (row_anchor * CC + col_anchor).reshape(-1).astype(jnp.int32)
    row_count = jnp.abs(row_offset)
    col_count = jnp.abs(col_offset)
    leftover = STEPS - row_count - col_count
    pairs_count = jax.random.randint(key_list[11], row_count.shape, 0, 1 << 20, dtype=jnp.int32) % (leftover // 2 + 1)
    vertical = jax.random.randint(key_list[12], row_count.shape, 0, 2, dtype=jnp.int32)
    moment = jnp.arange(STEPS, dtype=jnp.int32)[:, None, None]
    chosen = jnp.where(moment < row_count, jnp.where(row_offset > 0, 2, 1), jnp.where(moment < row_count + col_count, jnp.where(col_offset > 0, 4, 3), jnp.where(moment < row_count + col_count + pairs_count, jnp.where(vertical == 1, 1, 3), jnp.where(moment < row_count + col_count + 2 * pairs_count, jnp.where(vertical == 1, 2, 4), 0)))).astype(jnp.int32)
    shuffle = jax.random.randint(key_list[13], chosen.shape, 0, (1 << 30) // STEPS, dtype=jnp.int32) * STEPS + moment
    ordering = jnp.argsort(shuffle, axis=0)
    actions = jnp.take_along_axis(chosen, ordering, axis=0).reshape(STEPS, -1).astype(jnp.int32)
    return (start_cell, actions)


def draw_start_cell(key, part):
    return plan_agents(key)[0]


def draw_actions(key, part):
    return plan_agents(key)[1]


def with_ends(values, own_key, smallest, largest):
    place = [jax.random.randint(jax.random.fold_in(own_key, axis), (), 0, length) for axis, length in enumerate(values.shape)]
    widest = values.shape.index(max(values.shape))
    neighbour = place[:widest] + [(place[widest] + 1) % values.shape[widest]] + place[widest + 1:]
    return values.at[tuple(place)].set(smallest).at[tuple(neighbour)].set(largest)


def setup_inputs(seed: int = 0) -> dict:
    seeds = jax.random.split(jax.random.key(seed), 6)
    map_codes = with_ends(jax.random.randint(seeds[0], (NR, NC), 0, CODES), jax.random.fold_in(seeds[0], 1), 0, CODES - 1).astype(jnp.int32)
    reward_table = jnp.clip(jax.random.uniform(seeds[1], (TASKS, CODES), jnp.float32, -1.0, 1.0), -1.0, 1.0)
    start_cell = draw_start_cell(jax.random.fold_in(seeds[5], 71), 0)
    agent_task = with_ends(jax.random.randint(seeds[3], (AGENTS,), 0, TASKS), jax.random.fold_in(seeds[3], 1), 0, TASKS - 1).astype(jnp.int32)
    actions = draw_actions(jax.random.fold_in(seeds[5], 71), 0)
    return dict(map_codes=map_codes, reward_table=reward_table, start_cell=start_cell, agent_task=agent_task, actions=actions)


GAMMA = 0.95
PENALTY = 0.5


def sweep_cells(reward, living, padded):
    from_above = padded[..., :-2, 1:-1]
    from_below = padded[..., 2:, 1:-1]
    from_left = padded[..., 1:-1, :-2]
    from_right = padded[..., 1:-1, 2:]
    highest = jnp.maximum(jnp.maximum(from_above, from_below), jnp.maximum(from_left, from_right))
    return reward + GAMMA * living * highest


def reference(map_codes, reward_table, start_cell, agent_task, actions):
    row_moves = jnp.sum((actions == 2).astype(jnp.int32) - (actions == 1).astype(jnp.int32), axis=0)
    col_moves = jnp.sum((actions == 4).astype(jnp.int32) - (actions == 3).astype(jnp.int32), axis=0)
    slot_index = jnp.arange(AGENTS, dtype=jnp.int32)
    block_index = slot_index // AG_DEV
    tile_column = block_index // N_GY
    tile_row = block_index % N_GY
    final_row = (tile_row * CR + start_cell // CC + row_moves) % NR
    final_col = (tile_column * CC + start_cell % CC + col_moves) % NC
    final_cell = (final_row * NC + final_col).astype(jnp.int32)
    crowding = jnp.zeros((NR * NC,), jnp.float32).at[final_cell].add(1.0).reshape(NR, NC)
    living = (map_codes < CODES - TERMINAL).astype(jnp.float32)

    def solve_task(table_row):
        reward = table_row[map_codes] - PENALTY * crowding

        def one_sweep(sweep_index, current):
            padded = jnp.pad(current, ((1, 1), (1, 1)), mode="wrap")
            return sweep_cells(reward, living, padded)

        return lax.fori_loop(0, SWEEPS, one_sweep, reward)

    values = lax.map(solve_task, reward_table)
    flat_values = values.reshape(TASKS, NR * NC)
    agent_value = flat_values[agent_task, final_cell]
    return values, agent_value
```

```python
import functools

import jax
import jax.numpy as jnp
from jax import lax
from jax.experimental import pallas as pl
from jax.experimental.pallas import tpu as pltpu
from jax.sharding import PartitionSpec as P

SWEEPS = 16
CODES = 64
TERMINAL = 2
GAMMA = 0.95
PENALTY = 0.5
NEIGHBOURS = ((-1, -1), (-1, 0), (-1, 1), (0, -1), (0, 1), (1, -1), (1, 0), (1, 1))

TILE = 256
HALO = 32
EXT = TILE + 2 * HALO
ROWS = EXT // 8
COLS = 10
LANES = 128
TASK_LANES = 32
WIDE = COLS * LANES
AGENTS = 2048
STRIDE = 512
EDGE = 48

F32 = jnp.float32
BF16 = jnp.bfloat16
I32 = jnp.int32
MESH = pl.DeviceIdType.MESH
NT = (((1,), (1,)), ((), ()))
NN = (((1,), (0,)), ((), ()))


def dot(a, b, dims=NN):
    return lax.dot_general(a, b, dims, preferred_element_type=F32)


def iota(shape, dim):
    return lax.broadcasted_iota(I32, shape, dim)


def hot(values, first, count):
    cells = iota((count, values.shape[1]), 0) + first
    return jnp.where(cells == values, 1.0, 0.0).astype(BF16)


def edge_hot(cols):
    slot = iota((LANES, cols.shape[1]), 0)
    place = jnp.where(cols < EDGE, cols, cols - (EXT - EDGE) + EDGE)
    place = jnp.where((cols >= EDGE) & (cols < EXT - EDGE), -1, place)
    place = jnp.where((cols < 0) | (cols >= EXT), -1, place)
    return jnp.where(slot == place, 1.0, 0.0).astype(BF16)


def exchange_kernel(
    start_hbm, act_hbm, codes_hbm,
    cells_out, lists_out, n_out, s_out, w_out, e_out, corner_out,
    start_v, act_v, codes_v, w_send, e_send, corner_send, local_sem, send_sem, recv_sem,
):
    gx = lax.axis_index("gx")
    gy = lax.axis_index("gy")

    def device(step):
        return (lax.rem(gx + step[1] + 16, 16), lax.rem(gy + step[0] + 16, 16))

    loads = [
        pltpu.make_async_copy(codes_hbm, codes_v, local_sem.at[0]),
        pltpu.make_async_copy(act_hbm, act_v, local_sem.at[1]),
        pltpu.make_async_copy(start_hbm, start_v, local_sem.at[2]),
    ]
    for load in loads:
        load.start()
    barrier = pltpu.get_barrier_semaphore()
    for step in NEIGHBOURS:
        pl.semaphore_signal(barrier, inc=1, device_id=device(step), device_id_type=MESH)

    loads[1].wait()
    loads[2].wait()
    act = act_v[...]
    row = start_v[...] // TILE + HALO
    col = start_v[...] % TILE + HALO
    row += jnp.sum((act == 2).astype(I32) - (act == 1).astype(I32), axis=0, keepdims=True)
    col += jnp.sum((act == 4).astype(I32) - (act == 3).astype(I32), axis=0, keepdims=True)
    cells_out[...] = row * STRIDE + col

    loads[0].wait()
    lane = iota((64, LANES), 1)
    west = jnp.zeros((64, LANES), I32)
    east = jnp.zeros((64, LANES), I32)
    for q in range(4):
        mine = (lane >= 32 * q) & (lane < 32 * q + 32)
        rows = pl.ds(64 * q, 64)
        low = codes_v[rows, 0:128]
        high = codes_v[rows, 128:256]
        west = jnp.where(mine, pltpu.roll(low, 32 * q, 1), west)
        east = jnp.where(mine, pltpu.roll(high, (32 * q + 32) % 128, 1), east)
    w_send[...] = west
    e_send[...] = east
    for k, (r, c) in enumerate(((-1, -1), (-1, 1), (1, -1), (1, 1))):
        piece = jnp.zeros((8, LANES), I32)
        for q in range(4):
            mine = (lane[0:8] >= 32 * q) & (lane[0:8] < 32 * q + 32)
            rows = pl.ds((0 if r < 0 else 224) + 8 * q, 8)
            if c < 0:
                part = pltpu.roll(codes_v[rows, 0:128], 32 * q, 1)
            else:
                part = pltpu.roll(codes_v[rows, 128:256], (32 * q + 32) % 128, 1)
            piece = jnp.where(mine, part, piece)
        corner_send[k] = piece

    pl.semaphore_wait(barrier, 8)
    copies = []

    def send(source, target, step):
        k = len(copies)
        copy = pltpu.make_async_remote_copy(
            source, target, send_sem.at[k], recv_sem.at[k],
            device_id=device(step), device_id_type=MESH,
        )
        copy.start()
        copies.append(copy)

    send(w_send, e_out, (0, -1))
    send(e_send, w_out, (0, 1))
    for k, step in enumerate(((-1, -1), (-1, 1), (1, -1), (1, 1))):
        send(corner_send.at[k], corner_out.at[3 - k], step)
    for k, step in enumerate(NEIGHBOURS):
        send(cells_out, lists_out.at[7 - k], step)
    send(codes_v.at[pl.ds(0, 32)], s_out, (-1, 0))
    send(codes_v.at[pl.ds(224, 32)], n_out, (1, 0))
    for copy in copies:
        copy.wait()


def exchange(codes, start, actions):
    return pl.pallas_call(
        exchange_kernel,
        out_shape=(
            jax.ShapeDtypeStruct((1, AGENTS), I32),
            jax.ShapeDtypeStruct((8, 1, AGENTS), I32),
            jax.ShapeDtypeStruct((32, TILE), I32),
            jax.ShapeDtypeStruct((32, TILE), I32),
            jax.ShapeDtypeStruct((64, LANES), I32),
            jax.ShapeDtypeStruct((64, LANES), I32),
            jax.ShapeDtypeStruct((4, 8, LANES), I32),
        ),
        in_specs=[pl.BlockSpec(memory_space=pl.ANY)] * 3,
        out_specs=[pl.BlockSpec(memory_space=pltpu.VMEM)] * 7,
        scratch_shapes=[
            pltpu.VMEM((1, AGENTS), I32),
            pltpu.VMEM((16, AGENTS), I32),
            pltpu.VMEM((TILE, TILE), I32),
            pltpu.VMEM((64, LANES), I32),
            pltpu.VMEM((64, LANES), I32),
            pltpu.VMEM((4, 8, LANES), I32),
            pltpu.SemaphoreType.DMA((3,)),
            pltpu.SemaphoreType.DMA((16,)),
            pltpu.SemaphoreType.DMA((16,)),
        ],
        compiler_params=pltpu.CompilerParams(collective_id=0, has_side_effects=True),
        name="exchange",
    )(start, actions, codes)


def frame_kernel(
    cells_ref, lists_ref, n_ref, s_ref, w_ref, e_ref, corner_ref, codes_ref, table_ref, task_ref,
    values_out, agent_out,
    codes_v, count_v, reward_v, decay_v, val_a, val_b, natural_v, picked_v,
    index_v, index_s, out_sem, index_sem,
):
    cells = cells_ref[...]
    row = cells // STRIDE
    col = cells % STRIDE

    block = (row * 1639) >> 16
    inner = row - block * ROWS
    group = (col * 6554) >> 16
    place = ((inner + 1) * COLS + (col - group * COLS)) * 8 + block
    lane_of = task_ref[...] * TASK_LANES + group
    for k in range(16):
        index_v[k : k + 1, :] = place[:, k * LANES : (k + 1) * LANES]
    to_smem = pltpu.make_async_copy(index_v, index_s, index_sem)
    to_smem.start()

    lists = [lists_ref[k] for k in range(8)]
    rows_in = []
    cols_in = []
    for k, (r, c) in enumerate(NEIGHBOURS):
        rows_in.append(lists[k] // STRIDE + r * TILE)
        cols_in.append(lists[k] % STRIDE + c * TILE)
    row_hot = hot(row, 0, EXT)

    def add(k, first, rows, part, fresh=False):
        band = pl.ds(first, rows)
        for c in range(part.shape[1] // LANES):
            piece = part[:, c * LANES : (c + 1) * LANES]
            count_v[k + c, band, :] = piece if fresh else count_v[k + c, band, :] + piece

    def inside(columns):
        columns = jnp.where((columns >= EDGE) & (columns < EXT - EDGE), columns - EDGE, -1)
        return hot(columns, 0, 256)

    add(0, 0, EXT, dot(row_hot, inside(col), NT), True)
    sides = jnp.concatenate([row_hot, hot(rows_in[3], 0, EXT), hot(rows_in[4], 0, EXT)], axis=1)
    side_cols = jnp.concatenate([edge_hot(col), edge_hot(cols_in[3]), edge_hot(cols_in[4])], axis=1)
    add(2, 0, EXT, dot(sides, side_cols, NT), True)
    for first, west, middle, east in ((0, 0, 1, 2), (EXT - EDGE, 5, 6, 7)):
        near = hot(rows_in[middle], first, EDGE)
        add(0, first, EDGE, dot(near, inside(cols_in[middle]), NT))
        all_rows = jnp.concatenate(
            [near, hot(rows_in[west], first, EDGE), hot(rows_in[east], first, EDGE)], axis=1
        )
        all_cols = jnp.concatenate(
            [edge_hot(cols_in[middle]), edge_hot(cols_in[west]), edge_hot(cols_in[east])], axis=1
        )
        add(2, first, EDGE, dot(all_rows, all_cols, NT))

    for c in range(2):
        part = pl.ds(c * LANES, LANES)
        codes_v[c, 0:32, :] = n_ref[:, part].astype(F32)
        codes_v[c, 32:288, :] = codes_ref[:, part].astype(F32)
        codes_v[c, 288:320, :] = s_ref[:, part].astype(F32)
    lane = iota((64, LANES), 1)
    for q in range(4):
        west = pltpu.roll(w_ref[...], (128 - 32 * q) % 128, 1)
        east = pltpu.roll(e_ref[...], (160 - 32 * q) % 128, 1)
        both = jnp.where(lane < 32, west, jnp.where(lane < 64, east, 0))
        codes_v[2, 32 + 64 * q : 96 + 64 * q, :] = both.astype(F32)
        for first, pair in ((0, 0), (288, 2)):
            west = pltpu.roll(corner_ref[pair], (128 - 32 * q) % 128, 1)
            east = pltpu.roll(corner_ref[pair + 1], (160 - 32 * q) % 128, 1)
            both = jnp.where(lane[0:8] < 32, west, jnp.where(lane[0:8] < 64, east, 0))
            codes_v[2, first + 8 * q : first + 8 * q + 8, :] = both.astype(F32)

    out_lane = iota((384, WIDE), 1)
    column = (out_lane % TASK_LANES) * COLS + out_lane // LANES
    slot = iota((384, WIDE), 0)
    code_col = jnp.where(slot < 256, slot + HALO, jnp.where(slot < 288, slot - 256, slot))
    code_col = jnp.where(slot < 320, code_col, -1)
    spread_codes = jnp.where(code_col == column, 1.0, 0.0).astype(BF16)
    count_col = jnp.where(slot < 224, slot + EDGE, -1)
    count_col = jnp.where(slot >= 256, slot - 256, count_col)
    count_col = jnp.where(slot >= 256 + EDGE, slot - 256 - EDGE + EXT - EDGE, count_col)
    count_col = jnp.where(slot >= 256 + 2 * EDGE, -1, count_col)
    spread_counts = jnp.where(count_col == column, 1.0, 0.0).astype(BF16)

    def interleaved(ref):
        return jnp.concatenate(
            [
                jnp.concatenate([ref[c, pl.ds(i, 8, stride=ROWS), :] for i in range(ROWS)], axis=0)
                for c in range(3)
            ],
            axis=1,
        )

    counts = interleaved(count_v)
    high = jnp.floor(counts * (1.0 / 128.0))
    low = counts - high * 128.0
    minus = dot((high * (-128.0 * PENALTY)).astype(BF16), spread_counts)
    minus += dot((low * -PENALTY).astype(BF16), spread_counts)
    wide = dot(interleaved(codes_v).astype(BF16), spread_codes)

    lane8 = iota((8, LANES), 1)
    table = []
    for k in range(2):
        pair = jnp.concatenate([table_ref[2 * k : 2 * k + 1, :], table_ref[2 * k + 1 : 2 * k + 2, :]], axis=1)
        table.append(jnp.broadcast_to(pair, (8, LANES)))
    shift = (lane8 // TASK_LANES % 2) * CODES
    for i in range(ROWS):
        for j in range(COLS):
            code = wide[8 * i : 8 * i + 8, LANES * j : LANES * (j + 1)].astype(I32)
            at = code + shift
            found = jnp.where(
                lane8 < 64,
                jnp.take_along_axis(table[0], at, axis=1),
                jnp.take_along_axis(table[1], at, axis=1),
            )
            reward = found + minus[8 * i : 8 * i + 8, LANES * j : LANES * (j + 1)]
            spot = pl.ds((i * COLS + j) * 8, 8)
            reward_v[spot, :] = reward
            decay_v[spot, :] = jnp.where(code < CODES - TERMINAL, GAMMA, 0.0)
            val_a[pl.ds(((i + 1) * COLS + j) * 8, 8), :] = reward

    def take(ref, i):
        return [ref[pl.ds((i * COLS + j) * 8, 8), :] for j in range(COLS)]

    def put(ref, i, vregs):
        for j in range(COLS):
            ref[pl.ds((i * COLS + j) * 8, 8), :] = vregs[j]

    def wrap(ref):
        put(ref, 0, [pltpu.roll(x, 1, 0) for x in take(ref, ROWS)])
        put(ref, ROWS + 1, [pltpu.roll(x, 7, 0) for x in take(ref, 1)])

    def sides_of(now):
        return pltpu.roll(now[COLS - 1], 1, 1), pltpu.roll(now[0], LANES - 1, 1)

    def sweep(source, target):
        above, now = take(source, 0), take(source, 1)
        outer = sides_of(now)
        for i in range(ROWS):
            below = take(source, i + 2)
            left = [outer[0]] + now[:-1]
            right = now[1:] + [outer[1]]
            new = []
            for j in range(COLS):
                best = jnp.maximum(jnp.maximum(above[j], below[j]), jnp.maximum(left[j], right[j]))
                spot = pl.ds((i * COLS + j) * 8, 8)
                new.append(reward_v[spot, :] + decay_v[spot, :] * best)
            put(target, i + 1, new)
            above, now = now, below
            outer = sides_of(now)
        wrap(target)

    wrap(val_a)

    def two_sweeps(index, carry):
        sweep(val_a, val_b)
        sweep(val_b, val_a)
        return carry

    lax.fori_loop(0, SWEEPS // 2, two_sweeps, 0)

    block = jnp.concatenate(
        [
            jnp.concatenate(
                [val_a[pl.ds(((i + 1) * COLS + j) * 8, 8), :] for i in range(ROWS)], axis=0
            )
            for j in range(COLS)
        ],
        axis=1,
    )
    upper = block.astype(BF16)
    lower = (block - upper.astype(F32)).astype(BF16)
    in_lane = iota((WIDE, 4 * TILE), 0)
    spot = iota((WIDE, 4 * TILE), 1)
    column = (in_lane % TASK_LANES) * COLS + in_lane // LANES - HALO
    match = (column == spot % TILE) & (in_lane % LANES // TASK_LANES == spot // TILE)
    back = jnp.where(match, 1.0, 0.0).astype(BF16)
    flat = dot(upper, back) + dot(lower, back)
    for i in range(ROWS):
        for c in range(8):
            piece = flat[8 * i : 8 * i + 8, c * LANES : (c + 1) * LANES]
            natural_v[c, pl.ds(i, 8, stride=ROWS), :] = piece
    stores = []
    for c in range(8):
        stores.append(
            pltpu.make_async_copy(
                natural_v.at[c, pl.ds(HALO, TILE)],
                values_out.at[c // 2, :, pl.ds(c % 2 * LANES, LANES)],
                out_sem.at[c],
            )
        )
        stores[-1].start()

    to_smem.wait()

    def pick(k, carry):
        for a in range(LANES):
            picked_v[pl.ds(k * LANES + a, 1), :] = val_a[pl.ds(index_s[k, a], 1), :]
        return carry

    lax.fori_loop(0, 16, pick, 0)
    square = iota((LANES, LANES), 0)
    diagonal = square == iota((LANES, LANES), 1)
    for k in range(16):
        rows = picked_v[k * LANES : (k + 1) * LANES, :]
        upper = rows.astype(BF16)
        lower = (rows - upper.astype(F32)).astype(BF16)
        select = jnp.where(square == lane_of[:, k * LANES : (k + 1) * LANES], 1.0, 0.0).astype(BF16)
        crossed = dot(upper, select) + dot(lower, select)
        agent_out[:, k * LANES : (k + 1) * LANES] = jnp.sum(
            jnp.where(diagonal, crossed, 0.0), axis=0, keepdims=True
        )
    for store in stores:
        store.wait()


def frame(cells, lists, n, s, w, e, corner, codes, table, task):
    return pl.pallas_call(
        frame_kernel,
        out_shape=(
            jax.ShapeDtypeStruct((4, TILE, TILE), F32),
            jax.ShapeDtypeStruct((1, AGENTS), F32),
        ),
        in_specs=[pl.BlockSpec(memory_space=pltpu.VMEM)] * 10,
        out_specs=[pl.BlockSpec(memory_space=pl.ANY), pl.BlockSpec(memory_space=pltpu.VMEM)],
        scratch_shapes=[
            pltpu.VMEM((3, EXT, LANES), F32),
            pltpu.VMEM((3, EXT, LANES), F32),
            pltpu.VMEM((ROWS * COLS * 8, LANES), F32),
            pltpu.VMEM((ROWS * COLS * 8, LANES), F32),
            pltpu.VMEM(((ROWS + 2) * COLS * 8, LANES), F32),
            pltpu.VMEM(((ROWS + 2) * COLS * 8, LANES), F32),
            pltpu.VMEM((8, EXT, LANES), F32),
            pltpu.VMEM((AGENTS, LANES), F32),
            pltpu.VMEM((16, LANES), I32),
            pltpu.SMEM((16, LANES), I32),
            pltpu.SemaphoreType.DMA((8,)),
            pltpu.SemaphoreType.DMA,
        ],
        compiler_params=pltpu.CompilerParams(vmem_limit_bytes=40 << 20),
        name="frame",
    )(cells, lists, n, s, w, e, corner, codes, table, task)


def on_device(map_codes, reward_table, start_cell, agent_task, actions):
    arrived = exchange(map_codes, start_cell.reshape(1, AGENTS), actions)
    values, agent_value = frame(*arrived, map_codes, reward_table, agent_task.reshape(1, AGENTS))
    return values, agent_value.reshape(AGENTS)


def solution(mesh):
    placed = (P("gy", "gx"), P(), P(("gx", "gy")), P(("gx", "gy")), P(None, ("gx", "gy")))
    return jax.shard_map(
        on_device,
        mesh=mesh,
        in_specs=placed,
        out_specs=(P(None, "gy", "gx"), P(("gx", "gy"))),
        check_vma=False,
    )
```

```python
import functools

import jax
import jax.numpy as jnp
from jax import lax
from jax.experimental import pallas as pl
from jax.experimental.pallas import tpu as pltpu
from jax.sharding import PartitionSpec as P

SWEEPS = 16
CODES = 64
TERMINAL = 2
GAMMA = 0.95
PENALTY = 0.5
CORNERS = ((-1, -1), (-1, 1), (1, -1), (1, 1))
SIDES = ((-1, 0), (0, -1), (0, 1), (1, 0))
NEIGHBOURS = ((-1, -1), (-1, 0), (-1, 1), (0, -1), (0, 1), (1, -1), (1, 0), (1, 1))

TILE = 256
HALO = 32
EXT = TILE + 2 * HALO
ROWS = EXT // 8
COLS = 10
LANES = 128
TASK_LANES = 32
WIDE = COLS * LANES
AGENTS = 2048
STRIDE = 512
EDGE = 48
FAR = EXT - EDGE

F32 = jnp.float32
BF16 = jnp.bfloat16
F8 = jnp.float8_e4m3fn
I32 = jnp.int32
MESH = pl.DeviceIdType.MESH
NT = (((1,), (1,)), ((), ()))
NN = (((1,), (0,)), ((), ()))


def dot(a, b, dims=NN):
    return lax.dot_general(a, b, dims, preferred_element_type=F32)


def iota(shape, dim):
    return lax.broadcasted_iota(I32, shape, dim)


def one(match, kind):
    return jnp.where(match, 1.0, 0.0).astype(kind)


def hot(values, count):
    return one(iota((count, values.shape[1]), 0) == values, F8)


def slots(cols, low, high):
    near = (cols >= low) & (cols < low + EDGE)
    far = (cols >= high) & (cols < high + EDGE)
    return jnp.where(near, cols - low, jnp.where(far, cols - high + 64, -1))


def inner_slots(cols):
    return jnp.where((cols >= EDGE) & (cols < FAR), cols - EDGE, -1)


def exchange_kernel(
    start_hbm, act_hbm, codes_hbm, task_hbm,
    lists_out, n_out, s_out, w_out, e_out, corner_out, codes_out, count_out,
    spread_codes, spread_counts, back_out, index_out, select_out,
    start_v, act_v, task_v, cells_v, w_send, e_send, corner_send, local_sem, send_sem, recv_sem,
):
    gx = lax.axis_index("gx")
    gy = lax.axis_index("gy")

    def device(step):
        return (lax.rem(gx + step[1] + 16, 16), lax.rem(gy + step[0] + 16, 16))

    loads = [
        pltpu.make_async_copy(act_hbm, act_v, local_sem.at[0]),
        pltpu.make_async_copy(start_hbm, start_v, local_sem.at[1]),
        pltpu.make_async_copy(codes_hbm, codes_out, local_sem.at[2]),
        pltpu.make_async_copy(task_hbm, task_v, local_sem.at[3]),
    ]
    for load in loads:
        load.start()
    barrier = pltpu.get_barrier_semaphore()
    for step in NEIGHBOURS:
        pl.semaphore_signal(barrier, inc=1, device_id=device(step), device_id_type=MESH)

    loads[0].wait()
    loads[1].wait()
    act = act_v[...]
    start = start_v[...]
    row = (start >> 8) + HALO
    col = (start & 255) + HALO
    row += jnp.sum((act == 2).astype(I32) - (act == 1).astype(I32), axis=0, keepdims=True)
    col += jnp.sum((act == 4).astype(I32) - (act == 3).astype(I32), axis=0, keepdims=True)
    cells_v[...] = row * STRIDE + col

    targets = [hot(inner_slots(col), 256), hot(slots(col, 0, FAR), 128), hot(slots(col, 16, 256), 128)]
    own = dot(hot(row, EXT), jnp.concatenate(targets, axis=0), NT)
    for c in range(3):
        count_out[c] = own[:, c * LANES : (c + 1) * LANES]

    loads[2].wait()
    lane = iota((64, LANES), 1)
    west = jnp.zeros((64, LANES), I32)
    east = jnp.zeros((64, LANES), I32)
    for q in range(4):
        mine = (lane >= 32 * q) & (lane < 32 * q + 32)
        rows = pl.ds(64 * q, 64)
        west = jnp.where(mine, pltpu.roll(codes_out[rows, 0:128], 32 * q, 1), west)
        east = jnp.where(mine, pltpu.roll(codes_out[rows, 128:256], (32 * q + 32) % 128, 1), east)
    w_send[...] = west
    e_send[...] = east
    lane8 = iota((8, LANES), 1)
    lane24 = iota((24, LANES), 1)
    for k, (r, c) in enumerate(CORNERS):
        piece = jnp.zeros((8, LANES), I32)
        for q in range(4):
            mine = (lane8 >= 32 * q) & (lane8 < 32 * q + 32)
            rows = pl.ds((0 if r < 0 else 224) + 8 * q, 8)
            if c < 0:
                part = pltpu.roll(codes_out[rows, 0:128], 32 * q, 1)
            else:
                part = pltpu.roll(codes_out[rows, 128:256], (32 * q + 32) % 128, 1)
            piece = jnp.where(mine, part, piece)
        corner_send[k, 0:8, :] = piece
        first = 16 if r < 0 else 256
        upper = own[first : first + 24, 384:512]
        lower = own[first + 24 : first + 48, 384:512]
        if c < 0:
            lower = pltpu.roll(lower, 64, 1)
        else:
            upper = pltpu.roll(upper, 64, 1)
        corner_send[k, 8:32, :] = jnp.where(lane24 < 64, upper, lower).astype(I32)

    pl.semaphore_wait(barrier, 8)
    copies = []

    def send(source, target, step):
        k = len(copies)
        copy = pltpu.make_async_remote_copy(
            source, target, send_sem.at[k], recv_sem.at[k],
            device_id=device(step), device_id_type=MESH,
        )
        copy.start()
        copies.append(copy)

    send(w_send, e_out, (0, -1))
    send(e_send, w_out, (0, 1))
    for k, step in enumerate(CORNERS):
        send(corner_send.at[k], corner_out.at[3 - k], step)
    for k in (1, 2, 0, 3):
        send(cells_v, lists_out.at[3 - k], SIDES[k])
    send(codes_out.at[pl.ds(0, 32)], s_out, (-1, 0))
    send(codes_out.at[pl.ds(224, 32)], n_out, (1, 0))

    loads[3].wait()
    block = (row * 1639) >> 16
    group = (col * 6554) >> 16
    place = ((row - block * ROWS + 1) * COLS + (col - group * COLS)) * 8 + block
    lane_of = task_v[...] * TASK_LANES + group
    for k in range(16):
        part = slice(k * LANES, (k + 1) * LANES)
        index_out[k : k + 1, :] = place[:, part]
        select_out[:, part] = one(iota((LANES, LANES), 0) == lane_of[:, part], BF16)

    slot = iota((384, LANES), 0)
    code_col = jnp.where(slot < 256, slot + HALO, jnp.where(slot < 288, slot - 256, slot))
    code_col = jnp.where(slot < 320, code_col, -1)
    count_col = jnp.where(slot < FAR - EDGE, slot + EDGE, -1)
    count_col = jnp.where((slot >= 256) & (slot < 256 + EDGE), slot - 256, count_col)
    count_col = jnp.where((slot >= 320) & (slot < 320 + EDGE), slot - 320 + FAR, count_col)
    first_col = (iota((1, LANES), 1) & 31) * COLS
    in_lane = iota((LANES, LANES), 0)
    to_lane = iota((LANES, LANES), 1)
    for j in range(COLS):
        part = slice(j * LANES, (j + 1) * LANES)
        spread_codes[:, part] = one(code_col == first_col + j, BF16)
        spread_counts[:, part] = one(count_col == first_col + j, BF16)
        column = (in_lane & 31) * COLS + (j - HALO)
        column = jnp.where((column >= 0) & (column < TILE), column + (in_lane >> 5) * TILE, -1)
        for k in range(8):
            back_out[part, k * LANES : (k + 1) * LANES] = one(column == to_lane + k * LANES, BF16)
    for copy in copies:
        copy.wait()


def exchange(codes, start, actions, task):
    return pl.pallas_call(
        exchange_kernel,
        out_shape=(
            pltpu.VMEM((4, 1, AGENTS), I32),
            pltpu.VMEM((32, TILE), I32),
            pltpu.VMEM((32, TILE), I32),
            pltpu.VMEM((64, LANES), I32),
            pltpu.VMEM((64, LANES), I32),
            pltpu.VMEM((4, 32, LANES), I32),
            pltpu.VMEM((TILE, TILE), I32),
            pltpu.VMEM((3, EXT, LANES), F32),
            pltpu.VMEM((384, WIDE), BF16),
            pltpu.VMEM((384, WIDE), BF16),
            pltpu.VMEM((WIDE, 4 * TILE), BF16),
            pltpu.VMEM((16, LANES), I32),
            pltpu.VMEM((LANES, AGENTS), BF16),
        ),
        in_specs=[pl.BlockSpec(memory_space=pltpu.HBM)] * 4,
        out_specs=[pl.BlockSpec(memory_space=pltpu.VMEM)] * 13,
        scratch_shapes=[
            pltpu.VMEM((1, AGENTS), I32),
            pltpu.VMEM((16, AGENTS), I32),
            pltpu.VMEM((1, AGENTS), I32),
            pltpu.VMEM((1, AGENTS), I32),
            pltpu.VMEM((64, LANES), I32),
            pltpu.VMEM((64, LANES), I32),
            pltpu.VMEM((4, 32, LANES), I32),
            pltpu.SemaphoreType.DMA((4,)),
            pltpu.SemaphoreType.DMA((12,)),
            pltpu.SemaphoreType.DMA((12,)),
        ],
        compiler_params=pltpu.CompilerParams(
            collective_id=0, has_side_effects=True, vmem_limit_bytes=24 << 20
        ),
        name="exchange",
    )(start, actions, codes, task)


def frame_kernel(
    lists_ref, n_ref, s_ref, w_ref, e_ref, corner_ref, codes_ref, own_ref,
    spread_codes, spread_counts, back_ref, index_v, select_ref, table_hbm,
    values_out, agent_out,
    codes_v, count_v, reward_v, decay_v, val_a, val_b, natural_v, picked_v,
    index_s, table_ref, out_sem, index_sem, table_sem,
):
    to_smem = pltpu.make_async_copy(index_v, index_s, index_sem)
    to_smem.start()
    to_table = pltpu.make_async_copy(table_hbm, table_ref, table_sem)
    to_table.start()

    def cells_of(k):
        cells = lists_ref[k]
        step = SIDES[k]
        return (cells >> 9) + step[0] * TILE, (cells & (STRIDE - 1)) + step[1] * TILE

    row, col = cells_of(1)
    edges = own_ref[2] + dot(hot(row, EXT), hot(slots(col, 0, FAR), 128), NT)
    row, col = cells_of(2)
    count_v[2] = edges + dot(hot(row, EXT), hot(slots(col, 0, FAR), 128), NT)
    count_v[0] = own_ref[0]
    count_v[1] = own_ref[1]
    lane24 = iota((24, LANES), 1)
    for k, first, pair in ((0, 0, 0), (3, FAR, 2)):
        row, col = cells_of(k)
        targets = [hot(inner_slots(col), 256), hot(slots(col, 0, FAR), 128)]
        part = dot(hot(row - first, EDGE), jnp.concatenate(targets, axis=0), NT)
        band = slice(first, first + EDGE)
        for c in range(3):
            count_v[c, band, :] += part[:, c * LANES : (c + 1) * LANES]
        west = corner_ref[pair, 8:32, :].astype(F32)
        east = corner_ref[pair + 1, 8:32, :].astype(F32)
        west2 = pltpu.roll(west, 64, 1)
        east2 = pltpu.roll(east, 64, 1)
        count_v[2, first : first + 24, :] += jnp.where(lane24 < 64, west, east2)
        count_v[2, first + 24 : first + 48, :] += jnp.where(lane24 < 64, west2, east)

    for c in range(2):
        part = pl.ds(c * LANES, LANES)
        codes_v[c, 0:32, :] = n_ref[:, part].astype(F32)
        codes_v[c, 32:288, :] = codes_ref[:, part].astype(F32)
        codes_v[c, 288:320, :] = s_ref[:, part].astype(F32)
    lane = iota((64, LANES), 1)
    for q in range(4):
        west = pltpu.roll(w_ref[...], (128 - 32 * q) % 128, 1)
        east = pltpu.roll(e_ref[...], (160 - 32 * q) % 128, 1)
        both = jnp.where(lane < 32, west, jnp.where(lane < 64, east, 0))
        codes_v[2, 32 + 64 * q : 96 + 64 * q, :] = both.astype(F32)
        for first, pair in ((0, 0), (288, 2)):
            west = pltpu.roll(corner_ref[pair, 0:8, :], (128 - 32 * q) % 128, 1)
            east = pltpu.roll(corner_ref[pair + 1, 0:8, :], (160 - 32 * q) % 128, 1)
            both = jnp.where(lane[0:8] < 32, west, jnp.where(lane[0:8] < 64, east, 0))
            codes_v[2, first + 8 * q : first + 8 * q + 8, :] = both.astype(F32)

    def interleaved(ref):
        return jnp.concatenate(
            [
                jnp.concatenate([ref[c, pl.ds(i, 8, stride=ROWS), :] for i in range(ROWS)], axis=0)
                for c in range(3)
            ],
            axis=1,
        )

    counts = interleaved(count_v)
    high = jnp.floor(counts * (1.0 / 128.0))
    low = counts - high * 128.0
    minus = dot((high * (-128.0 * PENALTY)).astype(BF16), spread_counts[...])
    minus += dot((low * -PENALTY).astype(BF16), spread_counts[...])
    wide = dot(interleaved(codes_v).astype(BF16), spread_codes[...])

    to_table.wait()
    lane8 = iota((8, LANES), 1)
    table = []
    for k in range(2):
        pair = jnp.concatenate([table_ref[2 * k : 2 * k + 1, :], table_ref[2 * k + 1 : 2 * k + 2, :]], axis=1)
        table.append(jnp.broadcast_to(pair, (8, LANES)))
    shift = (lane8 // TASK_LANES % 2) * CODES
    for i in range(ROWS):
        for j in range(COLS):
            code = wide[8 * i : 8 * i + 8, LANES * j : LANES * (j + 1)].astype(I32)
            at = code + shift
            found = jnp.where(
                lane8 < 64,
                jnp.take_along_axis(table[0], at, axis=1),
                jnp.take_along_axis(table[1], at, axis=1),
            )
            reward = found + minus[8 * i : 8 * i + 8, LANES * j : LANES * (j + 1)]
            spot = pl.ds((i * COLS + j) * 8, 8)
            reward_v[spot, :] = reward
            decay_v[spot, :] = jnp.where(code < CODES - TERMINAL, GAMMA, 0.0)
            val_a[pl.ds(((i + 1) * COLS + j) * 8, 8), :] = reward

    def take(ref, i):
        return [ref[pl.ds((i * COLS + j) * 8, 8), :] for j in range(COLS)]

    def put(ref, i, vregs):
        for j in range(COLS):
            ref[pl.ds((i * COLS + j) * 8, 8), :] = vregs[j]

    def wrap(ref):
        put(ref, 0, [pltpu.roll(x, 1, 0) for x in take(ref, ROWS)])
        put(ref, ROWS + 1, [pltpu.roll(x, 7, 0) for x in take(ref, 1)])

    def sides_of(now):
        return pltpu.roll(now[COLS - 1], 1, 1), pltpu.roll(now[0], LANES - 1, 1)

    def sweep(source, target):
        above, now = take(source, 0), take(source, 1)
        outer = sides_of(now)
        for i in range(ROWS):
            below = take(source, i + 2)
            left = [outer[0]] + now[:-1]
            right = now[1:] + [outer[1]]
            new = []
            for j in range(COLS):
                best = jnp.maximum(jnp.maximum(above[j], below[j]), jnp.maximum(left[j], right[j]))
                spot = pl.ds((i * COLS + j) * 8, 8)
                new.append(reward_v[spot, :] + decay_v[spot, :] * best)
            put(target, i + 1, new)
            above, now = now, below
            outer = sides_of(now)
        wrap(target)

    wrap(val_a)

    def two_sweeps(index, carry):
        sweep(val_a, val_b)
        sweep(val_b, val_a)
        return carry

    lax.fori_loop(0, SWEEPS // 2, two_sweeps, 0)

    block = jnp.concatenate(
        [
            jnp.concatenate(
                [val_a[pl.ds(((i + 1) * COLS + j) * 8, 8), :] for i in range(ROWS)], axis=0
            )
            for j in range(COLS)
        ],
        axis=1,
    )
    upper = block.astype(BF16)
    lower = (block - upper.astype(F32)).astype(BF16)
    back = back_ref[...]
    flat = dot(upper, back) + dot(lower, back)
    for i in range(ROWS):
        for c in range(8):
            piece = flat[8 * i : 8 * i + 8, c * LANES : (c + 1) * LANES]
            natural_v[c, pl.ds(i, 8, stride=ROWS), :] = piece
    stores = []
    for c in range(8):
        stores.append(
            pltpu.make_async_copy(
                natural_v.at[c, pl.ds(HALO, TILE)],
                values_out.at[c // 2, :, pl.ds(c % 2 * LANES, LANES)],
                out_sem.at[c],
            )
        )
        stores[-1].start()

    to_smem.wait()

    def pick(k, carry):
        for a in range(LANES):
            picked_v[pl.ds(k * LANES + a, 1), :] = val_a[pl.ds(index_s[k, a], 1), :]
        return carry

    lax.fori_loop(0, 16, pick, 0)
    diagonal = iota((LANES, LANES), 0) == iota((LANES, LANES), 1)
    for k in range(16):
        rows = picked_v[k * LANES : (k + 1) * LANES, :]
        upper = rows.astype(BF16)
        lower = (rows - upper.astype(F32)).astype(BF16)
        select = select_ref[:, k * LANES : (k + 1) * LANES]
        crossed = dot(upper, select) + dot(lower, select)
        agent_out[:, k * LANES : (k + 1) * LANES] = jnp.sum(
            jnp.where(diagonal, crossed, 0.0), axis=0, keepdims=True
        )
    for store in stores:
        store.wait()


def frame(*arrays):
    return pl.pallas_call(
        frame_kernel,
        out_shape=(
            jax.ShapeDtypeStruct((4, TILE, TILE), F32),
            jax.ShapeDtypeStruct((1, AGENTS), F32),
        ),
        in_specs=[pl.BlockSpec(memory_space=pltpu.VMEM)] * 13 + [pl.BlockSpec(memory_space=pltpu.HBM)],
        out_specs=[pl.BlockSpec(memory_space=pltpu.HBM), pl.BlockSpec(memory_space=pltpu.VMEM)],
        scratch_shapes=[
            pltpu.VMEM((3, EXT, LANES), F32),
            pltpu.VMEM((3, EXT, LANES), F32),
            pltpu.VMEM((ROWS * COLS * 8, LANES), F32),
            pltpu.VMEM((ROWS * COLS * 8, LANES), F32),
            pltpu.VMEM(((ROWS + 2) * COLS * 8, LANES), F32),
            pltpu.VMEM(((ROWS + 2) * COLS * 8, LANES), F32),
            pltpu.VMEM((8, EXT, LANES), F32),
            pltpu.VMEM((AGENTS, LANES), F32),
            pltpu.SMEM((16, LANES), I32),
            pltpu.VMEM((4, CODES), F32),
            pltpu.SemaphoreType.DMA((8,)),
            pltpu.SemaphoreType.DMA,
            pltpu.SemaphoreType.DMA,
        ],
        compiler_params=pltpu.CompilerParams(vmem_limit_bytes=40 << 20),
        name="frame",
    )(*arrays)


def on_device(map_codes, reward_table, start_cell, agent_task, actions):
    arrived = exchange(
        map_codes, start_cell.reshape(1, AGENTS), actions, agent_task.reshape(1, AGENTS)
    )
    values, agent_value = frame(*arrived, reward_table)
    return values, agent_value.reshape(AGENTS)


def solution(mesh):
    placed = (P("gy", "gx"), P(), P(("gx", "gy")), P(("gx", "gy")), P(None, ("gx", "gy")))
    return jax.shard_map(
        on_device,
        mesh=mesh,
        in_specs=placed,
        out_specs=(P(None, "gy", "gx"), P(("gx", "gy"))),
        check_vma=False,
    )
```

```python
import functools

import jax
import jax.numpy as jnp
from jax import lax
from jax.experimental import pallas as pl
from jax.experimental.pallas import tpu as pltpu
from jax.sharding import PartitionSpec as P

SWEEPS = 16
CODES = 64
TERMINAL = 2
GAMMA = 0.95
PENALTY = 0.5
CORNERS = ((-1, -1), (-1, 1), (1, -1), (1, 1))
SIDES = ((-1, 0), (0, -1), (0, 1), (1, 0))
NEIGHBOURS = ((-1, -1), (-1, 0), (-1, 1), (0, -1), (0, 1), (1, -1), (1, 0), (1, 1))

TILE = 256
HALO = 32
EXT = TILE + 2 * HALO
ROWS = EXT // 8
COLS = 10
LANES = 128
TASK_LANES = 32
WIDE = COLS * LANES
AGENTS = 2048
STRIDE = 512
EDGE = 48
FAR = EXT - EDGE

F32 = jnp.float32
BF16 = jnp.bfloat16
F8 = jnp.float8_e4m3fn
I32 = jnp.int32
MESH = pl.DeviceIdType.MESH
NT = (((1,), (1,)), ((), ()))
NN = (((1,), (0,)), ((), ()))


def dot(a, b, dims=NN):
    return lax.dot_general(a, b, dims, preferred_element_type=F32)


def iota(shape, dim):
    return lax.broadcasted_iota(I32, shape, dim)


def one(match, kind):
    return jnp.where(match, 1.0, 0.0).astype(kind)


def hot(values, count):
    return one(iota((count, values.shape[1]), 0) == values, F8)


def slots(cols, low, high):
    near = (cols >= low) & (cols < low + EDGE)
    far = (cols >= high) & (cols < high + EDGE)
    return jnp.where(near, cols - low, jnp.where(far, cols - high + 64, -1))


def inner_slots(cols):
    return jnp.where((cols >= EDGE) & (cols < FAR), cols - EDGE, -1)


def exchange_kernel(
    start_hbm, act_hbm, codes_hbm, task_hbm,
    lists_out, n_out, s_out, w_out, e_out, corner_out, codes_out, count_out,
    spread_codes, spread_counts, back_out, index_out, select_out,
    start_v, act_v, task_v, cells_v, w_send, e_send, corner_send, local_sem, send_sem, recv_sem,
):
    gx = lax.axis_index("gx")
    gy = lax.axis_index("gy")

    def device(step):
        return (lax.rem(gx + step[1] + 16, 16), lax.rem(gy + step[0] + 16, 16))

    loads = [
        pltpu.make_async_copy(act_hbm, act_v, local_sem.at[0]),
        pltpu.make_async_copy(start_hbm, start_v, local_sem.at[1]),
        pltpu.make_async_copy(codes_hbm, codes_out, local_sem.at[2]),
        pltpu.make_async_copy(task_hbm, task_v, local_sem.at[3]),
    ]
    for load in loads:
        load.start()
    barrier = pltpu.get_barrier_semaphore()
    for step in NEIGHBOURS:
        pl.semaphore_signal(barrier, inc=1, device_id=device(step), device_id_type=MESH)

    loads[0].wait()
    loads[1].wait()
    act = act_v[...]
    start = start_v[...]
    row = (start >> 8) + HALO
    col = (start & 255) + HALO
    row += jnp.sum((act == 2).astype(I32) - (act == 1).astype(I32), axis=0, keepdims=True)
    col += jnp.sum((act == 4).astype(I32) - (act == 3).astype(I32), axis=0, keepdims=True)
    cells_v[...] = row * STRIDE + col

    targets = [hot(inner_slots(col), 256), hot(slots(col, 0, FAR), 128), hot(slots(col, 16, 256), 128)]
    own = dot(hot(row, EXT), jnp.concatenate(targets, axis=0), NT)
    for c in range(3):
        count_out[c] = own[:, c * LANES : (c + 1) * LANES]

    loads[2].wait()
    lane = iota((64, LANES), 1)
    west = jnp.zeros((64, LANES), I32)
    east = jnp.zeros((64, LANES), I32)
    for q in range(4):
        mine = (lane >= 32 * q) & (lane < 32 * q + 32)
        rows = pl.ds(64 * q, 64)
        west = jnp.where(mine, pltpu.roll(codes_out[rows, 0:128], 32 * q, 1), west)
        east = jnp.where(mine, pltpu.roll(codes_out[rows, 128:256], (32 * q + 32) % 128, 1), east)
    w_send[...] = west
    e_send[...] = east
    lane8 = iota((8, LANES), 1)
    lane24 = iota((24, LANES), 1)
    for k, (r, c) in enumerate(CORNERS):
        piece = jnp.zeros((8, LANES), I32)
        for q in range(4):
            mine = (lane8 >= 32 * q) & (lane8 < 32 * q + 32)
            rows = pl.ds((0 if r < 0 else 224) + 8 * q, 8)
            if c < 0:
                part = pltpu.roll(codes_out[rows, 0:128], 32 * q, 1)
            else:
                part = pltpu.roll(codes_out[rows, 128:256], (32 * q + 32) % 128, 1)
            piece = jnp.where(mine, part, piece)
        corner_send[k, 0:8, :] = piece
        first = 16 if r < 0 else 256
        upper = own[first : first + 24, 384:512]
        lower = own[first + 24 : first + 48, 384:512]
        if c < 0:
            lower = pltpu.roll(lower, 64, 1)
        else:
            upper = pltpu.roll(upper, 64, 1)
        corner_send[k, 8:32, :] = jnp.where(lane24 < 64, upper, lower).astype(I32)

    pl.semaphore_wait(barrier, 8)
    copies = []

    def send(source, target, step):
        k = len(copies)
        copy = pltpu.make_async_remote_copy(
            source, target, send_sem.at[k], recv_sem.at[k],
            device_id=device(step), device_id_type=MESH,
        )
        copy.start()
        copies.append(copy)

    send(w_send, e_out, (0, -1))
    send(e_send, w_out, (0, 1))
    for k, step in enumerate(CORNERS):
        send(corner_send.at[k], corner_out.at[3 - k], step)
    for k in (1, 2, 0, 3):
        send(cells_v, lists_out.at[3 - k], SIDES[k])
    send(codes_out.at[pl.ds(0, 32)], s_out, (-1, 0))
    send(codes_out.at[pl.ds(224, 32)], n_out, (1, 0))

    loads[3].wait()
    block = (row * 1639) >> 16
    group = (col * 6554) >> 16
    place = ((row - block * ROWS + 1) * COLS + (col - group * COLS)) * 8 + block
    lane_of = task_v[...] * TASK_LANES + group
    for k in range(16):
        part = slice(k * LANES, (k + 1) * LANES)
        index_out[k : k + 1, :] = place[:, part]
        select_out[:, part] = one(iota((LANES, LANES), 0) == lane_of[:, part], BF16)

    slot = iota((384, LANES), 0)
    code_col = jnp.where(slot < 256, slot + HALO, jnp.where(slot < 288, slot - 256, slot))
    code_col = jnp.where(slot < 320, code_col, -1)
    count_col = jnp.where(slot < FAR - EDGE, slot + EDGE, -1)
    count_col = jnp.where((slot >= 256) & (slot < 256 + EDGE), slot - 256, count_col)
    count_col = jnp.where((slot >= 320) & (slot < 320 + EDGE), slot - 320 + FAR, count_col)
    first_col = (iota((1, LANES), 1) & 31) * COLS
    in_lane = iota((LANES, LANES), 0)
    to_lane = iota((LANES, LANES), 1)
    for j in range(COLS):
        part = slice(j * LANES, (j + 1) * LANES)
        spread_codes[:, part] = one(code_col == first_col + j, BF16)
        spread_counts[:, part] = one(count_col == first_col + j, BF16)
        column = (in_lane & 31) * COLS + (j - HALO)
        column = jnp.where((column >= 0) & (column < TILE), column + (in_lane >> 5) * TILE, -1)
        for k in range(8):
            back_out[part, k * LANES : (k + 1) * LANES] = one(column == to_lane + k * LANES, BF16)
    for copy in copies:
        copy.wait()


def exchange(codes, start, actions, task):
    return pl.pallas_call(
        exchange_kernel,
        out_shape=(
            pltpu.VMEM((4, 1, AGENTS), I32),
            pltpu.VMEM((32, TILE), I32),
            pltpu.VMEM((32, TILE), I32),
            pltpu.VMEM((64, LANES), I32),
            pltpu.VMEM((64, LANES), I32),
            pltpu.VMEM((4, 32, LANES), I32),
            pltpu.VMEM((TILE, TILE), I32),
            pltpu.VMEM((3, EXT, LANES), F32),
            pltpu.VMEM((384, WIDE), BF16),
            pltpu.VMEM((384, WIDE), BF16),
            pltpu.VMEM((WIDE, 4 * TILE), BF16),
            pltpu.VMEM((16, LANES), I32),
            pltpu.VMEM((LANES, AGENTS), BF16),
        ),
        in_specs=[pl.BlockSpec(memory_space=pltpu.HBM)] * 4,
        out_specs=[pl.BlockSpec(memory_space=pltpu.VMEM)] * 13,
        scratch_shapes=[
            pltpu.VMEM((1, AGENTS), I32),
            pltpu.VMEM((16, AGENTS), I32),
            pltpu.VMEM((1, AGENTS), I32),
            pltpu.VMEM((1, AGENTS), I32),
            pltpu.VMEM((64, LANES), I32),
            pltpu.VMEM((64, LANES), I32),
            pltpu.VMEM((4, 32, LANES), I32),
            pltpu.SemaphoreType.DMA((4,)),
            pltpu.SemaphoreType.DMA((12,)),
            pltpu.SemaphoreType.DMA((12,)),
        ],
        compiler_params=pltpu.CompilerParams(
            collective_id=0, has_side_effects=True, vmem_limit_bytes=24 << 20
        ),
        name="exchange",
    )(*[pltpu.with_memory_space_constraint(x, pltpu.HBM) for x in (start, actions, codes, task)])


def frame_kernel(
    lists_ref, n_ref, s_ref, w_ref, e_ref, corner_ref, codes_ref, own_ref,
    spread_codes, spread_counts, back_ref, index_v, select_ref, table_hbm,
    values_out, agent_out,
    codes_v, count_v, reward_v, decay_v, val_a, val_b, natural_v, picked_v,
    index_s, table_ref, out_sem, index_sem, table_sem,
):
    to_smem = pltpu.make_async_copy(index_v, index_s, index_sem)
    to_smem.start()
    to_table = pltpu.make_async_copy(table_hbm, table_ref, table_sem)
    to_table.start()

    def cells_of(k):
        cells = lists_ref[k]
        step = SIDES[k]
        return (cells >> 9) + step[0] * TILE, (cells & (STRIDE - 1)) + step[1] * TILE

    row, col = cells_of(1)
    edges = own_ref[2] + dot(hot(row, EXT), hot(slots(col, 0, FAR), 128), NT)
    row, col = cells_of(2)
    count_v[2] = edges + dot(hot(row, EXT), hot(slots(col, 0, FAR), 128), NT)
    count_v[0] = own_ref[0]
    count_v[1] = own_ref[1]
    lane24 = iota((24, LANES), 1)
    for k, first, pair in ((0, 0, 0), (3, FAR, 2)):
        row, col = cells_of(k)
        targets = [hot(inner_slots(col), 256), hot(slots(col, 0, FAR), 128)]
        part = dot(hot(row - first, EDGE), jnp.concatenate(targets, axis=0), NT)
        band = slice(first, first + EDGE)
        for c in range(3):
            count_v[c, band, :] += part[:, c * LANES : (c + 1) * LANES]
        west = corner_ref[pair, 8:32, :].astype(F32)
        east = corner_ref[pair + 1, 8:32, :].astype(F32)
        west2 = pltpu.roll(west, 64, 1)
        east2 = pltpu.roll(east, 64, 1)
        count_v[2, first : first + 24, :] += jnp.where(lane24 < 64, west, east2)
        count_v[2, first + 24 : first + 48, :] += jnp.where(lane24 < 64, west2, east)

    for c in range(2):
        part = pl.ds(c * LANES, LANES)
        codes_v[c, 0:32, :] = n_ref[:, part].astype(F32)
        codes_v[c, 32:288, :] = codes_ref[:, part].astype(F32)
        codes_v[c, 288:320, :] = s_ref[:, part].astype(F32)
    lane = iota((64, LANES), 1)
    for q in range(4):
        west = pltpu.roll(w_ref[...], (128 - 32 * q) % 128, 1)
        east = pltpu.roll(e_ref[...], (160 - 32 * q) % 128, 1)
        both = jnp.where(lane < 32, west, jnp.where(lane < 64, east, 0))
        codes_v[2, 32 + 64 * q : 96 + 64 * q, :] = both.astype(F32)
        for first, pair in ((0, 0), (288, 2)):
            west = pltpu.roll(corner_ref[pair, 0:8, :], (128 - 32 * q) % 128, 1)
            east = pltpu.roll(corner_ref[pair + 1, 0:8, :], (160 - 32 * q) % 128, 1)
            both = jnp.where(lane[0:8] < 32, west, jnp.where(lane[0:8] < 64, east, 0))
            codes_v[2, first + 8 * q : first + 8 * q + 8, :] = both.astype(F32)

    def interleaved(ref):
        return jnp.concatenate(
            [
                jnp.concatenate([ref[c, pl.ds(i, 8, stride=ROWS), :] for i in range(ROWS)], axis=0)
                for c in range(3)
            ],
            axis=1,
        )

    counts = interleaved(count_v)
    high = jnp.floor(counts * (1.0 / 128.0))
    low = counts - high * 128.0
    minus = dot((high * (-128.0 * PENALTY)).astype(BF16), spread_counts[...])
    minus += dot((low * -PENALTY).astype(BF16), spread_counts[...])
    wide = dot(interleaved(codes_v).astype(BF16), spread_codes[...])

    to_table.wait()
    lane8 = iota((8, LANES), 1)
    table = []
    for k in range(2):
        pair = jnp.concatenate([table_ref[2 * k : 2 * k + 1, :], table_ref[2 * k + 1 : 2 * k + 2, :]], axis=1)
        table.append(jnp.broadcast_to(pair, (8, LANES)))
    shift = (lane8 // TASK_LANES % 2) * CODES
    for i in range(ROWS):
        for j in range(COLS):
            code = wide[8 * i : 8 * i + 8, LANES * j : LANES * (j + 1)].astype(I32)
            at = code + shift
            found = jnp.where(
                lane8 < 64,
                jnp.take_along_axis(table[0], at, axis=1),
                jnp.take_along_axis(table[1], at, axis=1),
            )
            reward = found + minus[8 * i : 8 * i + 8, LANES * j : LANES * (j + 1)]
            spot = pl.ds((i * COLS + j) * 8, 8)
            reward_v[spot, :] = reward
            decay_v[spot, :] = jnp.where(code < CODES - TERMINAL, GAMMA, 0.0)
            val_a[pl.ds(((i + 1) * COLS + j) * 8, 8), :] = reward

    def take(ref, i):
        return [ref[pl.ds((i * COLS + j) * 8, 8), :] for j in range(COLS)]

    def put(ref, i, vregs):
        for j in range(COLS):
            ref[pl.ds((i * COLS + j) * 8, 8), :] = vregs[j]

    def wrap(ref):
        put(ref, 0, [pltpu.roll(x, 1, 0) for x in take(ref, ROWS)])
        put(ref, ROWS + 1, [pltpu.roll(x, 7, 0) for x in take(ref, 1)])

    def sides_of(now):
        return pltpu.roll(now[COLS - 1], 1, 1), pltpu.roll(now[0], LANES - 1, 1)

    def sweep(source, target):
        above, now = take(source, 0), take(source, 1)
        outer = sides_of(now)
        for i in range(ROWS):
            below = take(source, i + 2)
            left = [outer[0]] + now[:-1]
            right = now[1:] + [outer[1]]
            new = []
            for j in range(COLS):
                best = jnp.maximum(jnp.maximum(above[j], below[j]), jnp.maximum(left[j], right[j]))
                spot = pl.ds((i * COLS + j) * 8, 8)
                new.append(reward_v[spot, :] + decay_v[spot, :] * best)
            put(target, i + 1, new)
            above, now = now, below
            outer = sides_of(now)
        wrap(target)

    wrap(val_a)

    def two_sweeps(index, carry):
        sweep(val_a, val_b)
        sweep(val_b, val_a)
        return carry

    lax.fori_loop(0, SWEEPS // 2, two_sweeps, 0)

    block = jnp.concatenate(
        [
            jnp.concatenate(
                [val_a[pl.ds(((i + 1) * COLS + j) * 8, 8), :] for i in range(ROWS)], axis=0
            )
            for j in range(COLS)
        ],
        axis=1,
    )
    upper = block.astype(BF16)
    lower = (block - upper.astype(F32)).astype(BF16)
    back = back_ref[...]
    flat = dot(upper, back) + dot(lower, back)
    for i in range(ROWS):
        for c in range(8):
            piece = flat[8 * i : 8 * i + 8, c * LANES : (c + 1) * LANES]
            natural_v[c, pl.ds(i, 8, stride=ROWS), :] = piece
    stores = []
    for c in range(8):
        stores.append(
            pltpu.make_async_copy(
                natural_v.at[c, pl.ds(HALO, TILE)],
                values_out.at[c // 2, :, pl.ds(c % 2 * LANES, LANES)],
                out_sem.at[c],
            )
        )
        stores[-1].start()

    to_smem.wait()

    def pick(k, carry):
        for a in range(LANES):
            picked_v[pl.ds(k * LANES + a, 1), :] = val_a[pl.ds(index_s[k, a], 1), :]
        return carry

    lax.fori_loop(0, 16, pick, 0)
    diagonal = iota((LANES, LANES), 0) == iota((LANES, LANES), 1)
    for k in range(16):
        rows = picked_v[k * LANES : (k + 1) * LANES, :]
        upper = rows.astype(BF16)
        lower = (rows - upper.astype(F32)).astype(BF16)
        select = select_ref[:, k * LANES : (k + 1) * LANES]
        crossed = dot(upper, select) + dot(lower, select)
        agent_out[:, k * LANES : (k + 1) * LANES] = jnp.sum(
            jnp.where(diagonal, crossed, 0.0), axis=0, keepdims=True
        )
    for store in stores:
        store.wait()


def frame(*arrays):
    return pl.pallas_call(
        frame_kernel,
        out_shape=(
            jax.ShapeDtypeStruct((4, TILE, TILE), F32),
            jax.ShapeDtypeStruct((1, AGENTS), F32),
        ),
        in_specs=[pl.BlockSpec(memory_space=pltpu.VMEM)] * 13 + [pl.BlockSpec(memory_space=pltpu.HBM)],
        out_specs=[pl.BlockSpec(memory_space=pltpu.HBM), pl.BlockSpec(memory_space=pltpu.VMEM)],
        scratch_shapes=[
            pltpu.VMEM((3, EXT, LANES), F32),
            pltpu.VMEM((3, EXT, LANES), F32),
            pltpu.VMEM((ROWS * COLS * 8, LANES), F32),
            pltpu.VMEM((ROWS * COLS * 8, LANES), F32),
            pltpu.VMEM(((ROWS + 2) * COLS * 8, LANES), F32),
            pltpu.VMEM(((ROWS + 2) * COLS * 8, LANES), F32),
            pltpu.VMEM((8, EXT, LANES), F32),
            pltpu.VMEM((AGENTS, LANES), F32),
            pltpu.SMEM((16, LANES), I32),
            pltpu.VMEM((4, CODES), F32),
            pltpu.SemaphoreType.DMA((8,)),
            pltpu.SemaphoreType.DMA,
            pltpu.SemaphoreType.DMA,
        ],
        compiler_params=pltpu.CompilerParams(vmem_limit_bytes=40 << 20),
        name="frame",
    )(*arrays)


def on_device(map_codes, reward_table, start_cell, agent_task, actions):
    arrived = exchange(
        map_codes, start_cell.reshape(1, AGENTS), actions, agent_task.reshape(1, AGENTS)
    )
    values, agent_value = frame(*arrived, pltpu.with_memory_space_constraint(reward_table, pltpu.HBM))
    return values, agent_value.reshape(AGENTS)


def solution(mesh):
    placed = (P("gy", "gx"), P(), P(("gx", "gy")), P(("gx", "gy")), P(None, ("gx", "gy")))
    return jax.shard_map(
        on_device,
        mesh=mesh,
        in_specs=placed,
        out_specs=(P(None, "gy", "gx"), P(("gx", "gy"))),
        check_vma=False,
    )
```

```python
import functools

import jax
import jax.numpy as jnp
from jax import lax
from jax.experimental import pallas as pl
from jax.experimental.pallas import tpu as pltpu
from jax.sharding import PartitionSpec as P

SWEEPS = 16
CODES = 64
TERMINAL = 2
GAMMA = 0.95
PENALTY = 0.5
CORNERS = ((-1, -1), (-1, 1), (1, -1), (1, 1))
SIDES = ((-1, 0), (0, -1), (0, 1), (1, 0))
NEIGHBOURS = ((-1, -1), (-1, 0), (-1, 1), (0, -1), (0, 1), (1, -1), (1, 0), (1, 1))

TILE = 256
HALO = 32
EXT = TILE + 2 * HALO
ROWS = EXT // 8
COLS = 10
LANES = 128
TASK_LANES = 32
WIDE = COLS * LANES
AGENTS = 2048
STRIDE = 512
EDGE = 48
FAR = EXT - EDGE

F32 = jnp.float32
BF16 = jnp.bfloat16
F8 = jnp.float8_e4m3fn
I32 = jnp.int32
MESH = pl.DeviceIdType.MESH
NT = (((1,), (1,)), ((), ()))
NN = (((1,), (0,)), ((), ()))


def dot(a, b, dims=NN):
    return lax.dot_general(a, b, dims, preferred_element_type=F32)


def iota(shape, dim):
    return lax.broadcasted_iota(I32, shape, dim)


def one(match, kind):
    return jnp.where(match, 1.0, 0.0).astype(kind)


def hot(values, count):
    return one(iota((count, values.shape[1]), 0) == values, F8)


def slots(cols, low, high):
    near = (cols >= low) & (cols < low + EDGE)
    far = (cols >= high) & (cols < high + EDGE)
    return jnp.where(near, cols - low, jnp.where(far, cols - high + 64, -1))


def inner_slots(cols):
    return jnp.where((cols >= EDGE) & (cols < FAR), cols - EDGE, -1)


def interleaved(ref, tiles):
    parts = []
    for c in range(tiles):
        rows = [ref[c, pl.ds(i, 8, stride=ROWS), :] for i in range(ROWS)]
        parts.append(jnp.concatenate(rows, axis=0))
    return jnp.concatenate(parts, axis=1)


def limbs(counts):
    high = jnp.floor(counts * (1.0 / 128.0))
    low = counts - high * 128.0
    return (high * (-128.0 * PENALTY)).astype(BF16), (low * -PENALTY).astype(BF16)


def exchange_kernel(
    start_hbm, act_hbm, codes_hbm, task_hbm,
    side_out, w_out, e_out, corner_out, edge_out, code_out, minus_out,
    spread_codes, spread_counts, back_out, index_out, select_out,
    lists_v, n_v, s_v, codes_v, count_v, wide_v, start_v, act_v, task_v, cells_v, w_send, e_send, corner_send, local_sem, send_sem, recv_sem,
):
    gx = lax.axis_index("gx")
    gy = lax.axis_index("gy")

    def device(step):
        return (lax.rem(gx + step[1] + 16, 16), lax.rem(gy + step[0] + 16, 16))

    loads = [
        pltpu.make_async_copy(act_hbm, act_v, local_sem.at[0]),
        pltpu.make_async_copy(start_hbm, start_v, local_sem.at[1]),
        pltpu.make_async_copy(codes_hbm, codes_v, local_sem.at[2]),
        pltpu.make_async_copy(task_hbm, task_v, local_sem.at[3]),
    ]
    for load in loads:
        load.start()
    barrier = pltpu.get_barrier_semaphore()
    for step in NEIGHBOURS:
        pl.semaphore_signal(barrier, inc=1, device_id=device(step), device_id_type=MESH)

    loads[0].wait()
    loads[1].wait()
    act = act_v[...]
    start = start_v[...]
    row = (start >> 8) + HALO
    col = (start & 255) + HALO
    row += jnp.sum((act == 2).astype(I32) - (act == 1).astype(I32), axis=0, keepdims=True)
    col += jnp.sum((act == 4).astype(I32) - (act == 3).astype(I32), axis=0, keepdims=True)
    cells_v[...] = row * STRIDE + col

    loads[2].wait()
    lane = iota((64, LANES), 1)
    west = jnp.zeros((64, LANES), I32)
    east = jnp.zeros((64, LANES), I32)
    for q in range(4):
        mine = (lane >= 32 * q) & (lane < 32 * q + 32)
        rows = pl.ds(64 * q, 64)
        west = jnp.where(mine, pltpu.roll(codes_v[rows, 0:128], 32 * q, 1), west)
        east = jnp.where(mine, pltpu.roll(codes_v[rows, 128:256], (32 * q + 32) % 128, 1), east)
    w_send[...] = west
    e_send[...] = east
    pl.semaphore_wait(barrier, 8)
    copies = []

    def send(source, target, step):
        k = len(copies)
        copy = pltpu.make_async_remote_copy(
            source, target, send_sem.at[k], recv_sem.at[k],
            device_id=device(step), device_id_type=MESH,
        )
        copy.start()
        copies.append(copy)

    send(cells_v, side_out.at[1], (0, -1))
    send(cells_v, side_out.at[0], (0, 1))
    send(w_send, e_out, (0, -1))
    send(e_send, w_out, (0, 1))
    send(cells_v, lists_v.at[1], (-1, 0))
    send(cells_v, lists_v.at[0], (1, 0))
    send(codes_v.at[pl.ds(0, 32)], s_v, (-1, 0))
    send(codes_v.at[pl.ds(224, 32)], n_v, (1, 0))

    targets = [hot(inner_slots(col), 256), hot(slots(col, 0, FAR), 128), hot(slots(col, 16, 256), 128)]
    own = dot(hot(row, EXT), jnp.concatenate(targets, axis=0), NT)
    for c in range(2):
        count_v[c] = own[:, c * LANES : (c + 1) * LANES]
    edge_out[...] = own[:, 256:384]

    lane8 = iota((8, LANES), 1)
    lane24 = iota((24, LANES), 1)
    for k, (r, c) in enumerate(CORNERS):
        piece = jnp.zeros((8, LANES), I32)
        for q in range(4):
            mine = (lane8 >= 32 * q) & (lane8 < 32 * q + 32)
            rows = pl.ds((0 if r < 0 else 224) + 8 * q, 8)
            if c < 0:
                part = pltpu.roll(codes_v[rows, 0:128], 32 * q, 1)
            else:
                part = pltpu.roll(codes_v[rows, 128:256], (32 * q + 32) % 128, 1)
            piece = jnp.where(mine, part, piece)
        corner_send[k, 0:8, :] = piece
        first = 16 if r < 0 else 256
        upper = own[first : first + 24, 384:512]
        lower = own[first + 24 : first + 48, 384:512]
        if c < 0:
            lower = pltpu.roll(lower, 64, 1)
        else:
            upper = pltpu.roll(upper, 64, 1)
        corner_send[k, 8:32, :] = jnp.where(lane24 < 64, upper, lower).astype(I32)

    for k, step in enumerate(CORNERS):
        send(corner_send.at[k], corner_out.at[3 - k], step)

    loads[3].wait()
    block = (row * 1639) >> 16
    group = (col * 6554) >> 16
    place = ((row - block * ROWS + 1) * COLS + (col - group * COLS)) * 8 + block
    lane_of = task_v[...] * TASK_LANES + group
    for k in range(16):
        part = slice(k * LANES, (k + 1) * LANES)
        index_out[k : k + 1, :] = place[:, part]
        select_out[part, :] = jnp.broadcast_to(lane_of[:, part], (LANES, LANES)).T

    slot = iota((384, LANES), 0)
    code_col = jnp.where(slot < 256, slot + HALO, jnp.where(slot < 288, slot - 256, slot))
    code_col = jnp.where(slot < 320, code_col, -1)
    count_col = jnp.where(slot < FAR - EDGE, slot + EDGE, -1)
    count_col = jnp.where((slot >= 256) & (slot < 256 + EDGE), slot - 256, count_col)
    count_col = jnp.where((slot >= 320) & (slot < 320 + EDGE), slot - 320 + FAR, count_col)
    first_col = (iota((1, LANES), 1) & 31) * COLS
    in_lane = iota((LANES, LANES), 0)
    to_lane = iota((LANES, LANES), 1)
    for j in range(COLS):
        part = slice(j * LANES, (j + 1) * LANES)
        spread_codes[:, part] = one(code_col == first_col + j, BF16)
        spread_counts[:, part] = one(count_col == first_col + j, BF16)
        column = (in_lane & 31) * COLS + (j - HALO)
        column = jnp.where((column >= 0) & (column < TILE), column + (in_lane >> 5) * TILE, -1)
        for k in range(8):
            back_out[part, k * LANES : (k + 1) * LANES] = one(column == to_lane + k * LANES, BF16)

    for copy in copies[4:8]:
        copy.wait_recv()
    for k, first, step in ((0, 0, -1), (1, FAR, 1)):
        cells = lists_v[k]
        row = (cells >> 9) + step * TILE
        col = cells & (STRIDE - 1)
        targets = [hot(inner_slots(col), 256), hot(slots(col, 0, FAR), 128)]
        part = dot(hot(row - first, EDGE), jnp.concatenate(targets, axis=0), NT)
        band = slice(first, first + EDGE)
        for c in range(2):
            count_v[c, band, :] += part[:, c * LANES : (c + 1) * LANES]
        edge_out[band, :] += part[:, 256:384]
    for c in range(2):
        part = slice(c * LANES, (c + 1) * LANES)
        wide_v[c, 0:32, :] = n_v[:, part].astype(F32)
        wide_v[c, 32:288, :] = codes_v[:, part].astype(F32)
        wide_v[c, 288:320, :] = s_v[:, part].astype(F32)
    high, low = limbs(interleaved(count_v, 2))
    minus_out[...] = dot(high, spread_counts[0:256, :]) + dot(low, spread_counts[0:256, :])
    code_out[...] = dot(interleaved(wide_v, 2).astype(BF16), spread_codes[0:256, :])
    for k, copy in enumerate(copies):
        if not 4 <= k < 8:
            copy.wait_recv()
    for copy in copies:
        copy.wait_send()


def exchange(codes, start, actions, task):
    return pl.pallas_call(
        exchange_kernel,
        out_shape=(
            pltpu.VMEM((2, 1, AGENTS), I32),
            pltpu.VMEM((64, LANES), I32),
            pltpu.VMEM((64, LANES), I32),
            pltpu.VMEM((4, 32, LANES), I32),
            pltpu.VMEM((EXT, LANES), F32),
            pltpu.VMEM((EXT, WIDE), F32),
            pltpu.VMEM((EXT, WIDE), F32),
            pltpu.VMEM((384, WIDE), BF16),
            pltpu.VMEM((384, WIDE), BF16),
            pltpu.VMEM((WIDE, 4 * TILE), BF16),
            pltpu.VMEM((16, LANES), I32),
            pltpu.VMEM((AGENTS, LANES), I32),
        ),
        in_specs=[pl.BlockSpec(memory_space=pltpu.HBM)] * 4,
        out_specs=[pl.BlockSpec(memory_space=pltpu.VMEM)] * 12,
        scratch_shapes=[
            pltpu.VMEM((2, 1, AGENTS), I32),
            pltpu.VMEM((32, TILE), I32),
            pltpu.VMEM((32, TILE), I32),
            pltpu.VMEM((TILE, TILE), I32),
            pltpu.VMEM((2, EXT, LANES), F32),
            pltpu.VMEM((2, EXT, LANES), F32),
            pltpu.VMEM((1, AGENTS), I32),
            pltpu.VMEM((16, AGENTS), I32),
            pltpu.VMEM((1, AGENTS), I32),
            pltpu.VMEM((1, AGENTS), I32),
            pltpu.VMEM((64, LANES), I32),
            pltpu.VMEM((64, LANES), I32),
            pltpu.VMEM((4, 32, LANES), I32),
            pltpu.SemaphoreType.DMA((4,)),
            pltpu.SemaphoreType.DMA((12,)),
            pltpu.SemaphoreType.DMA((12,)),
        ],
        compiler_params=pltpu.CompilerParams(
            collective_id=0, has_side_effects=True, vmem_limit_bytes=24 << 20
        ),
        name="exchange",
    )(*[pltpu.with_memory_space_constraint(x, pltpu.HBM) for x in (start, actions, codes, task)])


def frame_kernel(
    lists_ref, w_ref, e_ref, corner_ref, own_ref, code_ref, minus_ref,
    spread_codes, spread_counts, back_ref, index_v, select_ref, table_hbm,
    values_out, agent_out,
    edge_v, reward_v, decay_v, val_a, val_b, natural_v, picked_v,
    index_s, table_ref, out_sem, index_sem, table_sem,
):
    to_smem = pltpu.make_async_copy(index_v, index_s, index_sem)
    to_smem.start()
    to_table = pltpu.make_async_copy(table_hbm, table_ref, table_sem)
    to_table.start()

    edges = own_ref[...]
    for k, step in ((0, -1), (1, 1)):
        cells = lists_ref[k]
        row = cells >> 9
        col = (cells & (STRIDE - 1)) + step * TILE
        edges += dot(hot(row, EXT), hot(slots(col, 0, FAR), 128), NT)
    edge_v[0] = edges
    lane24 = iota((24, LANES), 1)
    for first, pair_at in ((0, 0), (FAR, 2)):
        west = corner_ref[pair_at, 8:32, :].astype(F32)
        east = corner_ref[pair_at + 1, 8:32, :].astype(F32)
        west2 = pltpu.roll(west, 64, 1)
        east2 = pltpu.roll(east, 64, 1)
        edge_v[0, first : first + 24, :] += jnp.where(lane24 < 64, west, east2)
        edge_v[0, first + 24 : first + 48, :] += jnp.where(lane24 < 64, west2, east)

    lane = iota((64, LANES), 1)
    for q in range(4):
        west = pltpu.roll(w_ref[...], (128 - 32 * q) % 128, 1)
        east = pltpu.roll(e_ref[...], (160 - 32 * q) % 128, 1)
        both = jnp.where(lane < 32, west, jnp.where(lane < 64, east, 0))
        edge_v[1, 32 + 64 * q : 96 + 64 * q, :] = both.astype(F32)
        for first, pair_at in ((0, 0), (288, 2)):
            west = pltpu.roll(corner_ref[pair_at, 0:8, :], (128 - 32 * q) % 128, 1)
            east = pltpu.roll(corner_ref[pair_at + 1, 0:8, :], (160 - 32 * q) % 128, 1)
            both = jnp.where(lane[0:8] < 32, west, jnp.where(lane[0:8] < 64, east, 0))
            edge_v[1, first + 8 * q : first + 8 * q + 8, :] = both.astype(F32)

    last = interleaved(edge_v, 2)
    high, low = limbs(last[:, 0:LANES])
    spread = spread_counts[256:384, :]
    minus = dot(jnp.concatenate([high, low], axis=1), jnp.concatenate([spread, spread], axis=0))
    wide = dot(last[:, LANES:].astype(BF16), spread_codes[256:384, :])

    to_table.wait()
    lane8 = iota((8, LANES), 1)
    table = []
    for k in range(2):
        pair = jnp.concatenate([table_ref[2 * k : 2 * k + 1, :], table_ref[2 * k + 1 : 2 * k + 2, :]], axis=1)
        table.append(jnp.broadcast_to(pair, (8, LANES)))
    shift = (lane8 // TASK_LANES % 2) * CODES
    for i in range(ROWS):
        for j in range(COLS):
            block = slice(8 * i, 8 * i + 8), slice(LANES * j, LANES * (j + 1))
            code = (wide[block] + code_ref[block]).astype(I32)
            at = code + shift
            found = jnp.where(
                lane8 < 64,
                jnp.take_along_axis(table[0], at, axis=1),
                jnp.take_along_axis(table[1], at, axis=1),
            )
            reward = found + (minus[block] + minus_ref[block])
            spot = pl.ds((i * COLS + j) * 8, 8)
            reward_v[spot, :] = reward
            decay_v[spot, :] = jnp.where(code < CODES - TERMINAL, GAMMA, 0.0)
            val_a[pl.ds(((i + 1) * COLS + j) * 8, 8), :] = reward

    def take(ref, i):
        return [ref[pl.ds((i * COLS + j) * 8, 8), :] for j in range(COLS)]

    def put(ref, i, vregs):
        for j in range(COLS):
            ref[pl.ds((i * COLS + j) * 8, 8), :] = vregs[j]

    def wrap(ref):
        put(ref, 0, [pltpu.roll(x, 1, 0) for x in take(ref, ROWS)])
        put(ref, ROWS + 1, [pltpu.roll(x, 7, 0) for x in take(ref, 1)])

    def pair(above, now):
        right = now[1:] + [pltpu.roll(now[0], LANES - 1, 1)]
        return [jnp.maximum(a, b) for a, b in zip(above, right)]

    def sweep(source, target):
        now = take(source, 1)
        here = pair(take(source, 0), now)
        for i in range(ROWS):
            below = take(source, i + 2)
            under = pair(now, below)
            other = [pltpu.roll(under[COLS - 1], 1, 1)] + under[:-1]
            new = []
            for j in range(COLS):
                spot = pl.ds((i * COLS + j) * 8, 8)
                best = jnp.maximum(here[j], other[j])
                new.append(reward_v[spot, :] + decay_v[spot, :] * best)
            put(target, i + 1, new)
            now, here = below, under
        wrap(target)

    wrap(val_a)

    def two_sweeps(index, carry):
        sweep(val_a, val_b)
        sweep(val_b, val_a)
        return carry

    lax.fori_loop(0, SWEEPS // 2, two_sweeps, 0)

    block = jnp.concatenate(
        [
            jnp.concatenate(
                [val_a[pl.ds(((i + 1) * COLS + j) * 8, 8), :] for i in range(ROWS)], axis=0
            )
            for j in range(COLS)
        ],
        axis=1,
    )
    upper = block.astype(BF16)
    lower = (block - upper.astype(F32)).astype(BF16)
    back = back_ref[...]
    flat = dot(upper, back) + dot(lower, back)
    for i in range(ROWS):
        for c in range(8):
            piece = flat[8 * i : 8 * i + 8, c * LANES : (c + 1) * LANES]
            natural_v[c, pl.ds(i, 8, stride=ROWS), :] = piece
    stores = []
    for c in range(8):
        stores.append(
            pltpu.make_async_copy(
                natural_v.at[c, pl.ds(HALO, TILE)],
                values_out.at[c // 2, :, pl.ds(c % 2 * LANES, LANES)],
                out_sem.at[c],
            )
        )
        stores[-1].start()

    to_smem.wait()

    def pick(k, carry):
        for a in range(LANES):
            picked_v[pl.ds(k * LANES + a, 1), :] = val_a[pl.ds(index_s[k, a], 1), :]
        return carry

    lax.fori_loop(0, 16, pick, 0)
    diagonal = iota((LANES, LANES), 0) == iota((LANES, LANES), 1)
    for k in range(16):
        part = slice(k * LANES, (k + 1) * LANES)
        found = jnp.concatenate(
            [
                jnp.take_along_axis(
                    picked_v[k * LANES + 8 * a : k * LANES + 8 * a + 8, :],
                    select_ref[k * LANES + 8 * a : k * LANES + 8 * a + 8, :],
                    axis=1,
                )
                for a in range(16)
            ],
            axis=0,
        )
        agent_out[:, part] = jnp.sum(jnp.where(diagonal, found, 0.0), axis=0, keepdims=True)
    for store in stores:
        store.wait()


def frame(*arrays):
    return pl.pallas_call(
        frame_kernel,
        out_shape=(
            jax.ShapeDtypeStruct((4, TILE, TILE), F32),
            jax.ShapeDtypeStruct((1, AGENTS), F32),
        ),
        in_specs=[pl.BlockSpec(memory_space=pltpu.VMEM)] * 12 + [pl.BlockSpec(memory_space=pltpu.HBM)],
        out_specs=[pl.BlockSpec(memory_space=pltpu.HBM), pl.BlockSpec(memory_space=pltpu.VMEM)],
        scratch_shapes=[
            pltpu.VMEM((2, EXT, LANES), F32),
            pltpu.VMEM((ROWS * COLS * 8, LANES), F32),
            pltpu.VMEM((ROWS * COLS * 8, LANES), F32),
            pltpu.VMEM(((ROWS + 2) * COLS * 8, LANES), F32),
            pltpu.VMEM(((ROWS + 2) * COLS * 8, LANES), F32),
            pltpu.VMEM((8, EXT, LANES), F32),
            pltpu.VMEM((AGENTS, LANES), F32),
            pltpu.SMEM((16, LANES), I32),
            pltpu.VMEM((4, CODES), F32),
            pltpu.SemaphoreType.DMA((8,)),
            pltpu.SemaphoreType.DMA,
            pltpu.SemaphoreType.DMA,
        ],
        compiler_params=pltpu.CompilerParams(vmem_limit_bytes=40 << 20),
        name="frame",
    )(*arrays)


def on_device(map_codes, reward_table, start_cell, agent_task, actions):
    arrived = exchange(
        map_codes, start_cell.reshape(1, AGENTS), actions, agent_task.reshape(1, AGENTS)
    )
    values, agent_value = frame(*arrived, pltpu.with_memory_space_constraint(reward_table, pltpu.HBM))
    return values, agent_value.reshape(AGENTS)


def solution(mesh):
    placed = (P("gy", "gx"), P(), P(("gx", "gy")), P(("gx", "gy")), P(None, ("gx", "gy")))
    return jax.shard_map(
        on_device,
        mesh=mesh,
        in_specs=placed,
        out_specs=(P(None, "gy", "gx"), P(("gx", "gy"))),
        check_vma=False,
    )
```

```python
import functools

import jax
import jax.numpy as jnp
from jax import lax
from jax.experimental import pallas as pl
from jax.experimental.pallas import tpu as pltpu
from jax.sharding import PartitionSpec as P

SWEEPS = 16
CODES = 64
TERMINAL = 2
GAMMA = 0.95
PENALTY = 0.5
CORNERS = ((-1, -1), (-1, 1), (1, -1), (1, 1))
SIDES = ((-1, 0), (0, -1), (0, 1), (1, 0))
NEIGHBOURS = ((-1, -1), (-1, 0), (-1, 1), (0, -1), (0, 1), (1, -1), (1, 0), (1, 1))

TILE = 256
HALO = 32
EXT = TILE + 2 * HALO
ROWS = EXT // 8
COLS = 5
LANES = 128
TASK_LANES = 64
WIDE = COLS * LANES
BOTH = 2 * COLS
AGENTS = 2048
STRIDE = 512
EDGE = 48
FAR = EXT - EDGE

F32 = jnp.float32
BF16 = jnp.bfloat16
F8 = jnp.float8_e4m3fn
I32 = jnp.int32
MESH = pl.DeviceIdType.MESH
NT = (((1,), (1,)), ((), ()))
NN = (((1,), (0,)), ((), ()))


def dot(a, b, dims=NN):
    return lax.dot_general(a, b, dims, preferred_element_type=F32)


def iota(shape, dim):
    return lax.broadcasted_iota(I32, shape, dim)


def one(match, kind):
    return jnp.where(match, 1.0, 0.0).astype(kind)


def hot(values, count):
    return one(iota((count, values.shape[1]), 0) == values, F8)


def slots(cols, low, high):
    near = (cols >= low) & (cols < low + EDGE)
    far = (cols >= high) & (cols < high + EDGE)
    return jnp.where(near, cols - low, jnp.where(far, cols - high + 64, -1))


def inner_slots(cols):
    return jnp.where((cols >= EDGE) & (cols < FAR), cols - EDGE, -1)


def interleaved(ref, tiles):
    parts = []
    for c in range(tiles):
        rows = [ref[c, pl.ds(i, 8, stride=ROWS), :] for i in range(ROWS)]
        parts.append(jnp.concatenate(rows, axis=0))
    return jnp.concatenate(parts, axis=1)


def limbs(counts):
    high = jnp.floor(counts * (1.0 / 128.0))
    low = counts - high * 128.0
    return (high * (-128.0 * PENALTY)).astype(BF16), (low * -PENALTY).astype(BF16)


def exchange_kernel(
    start_hbm, act_hbm, codes_hbm, task_hbm,
    side_out, w_out, e_out, corner_out, edge_out, code_out, minus_out,
    spread_codes, spread_counts, back_out, index_out, select_out,
    lists_v, n_v, s_v, codes_v, count_v, wide_v, start_v, act_v, task_v, cells_v, w_send, e_send, corner_send, local_sem, send_sem, recv_sem,
):
    gx = lax.axis_index("gx")
    gy = lax.axis_index("gy")

    def device(step):
        return (lax.rem(gx + step[1] + 16, 16), lax.rem(gy + step[0] + 16, 16))

    loads = [
        pltpu.make_async_copy(act_hbm, act_v, local_sem.at[0]),
        pltpu.make_async_copy(start_hbm, start_v, local_sem.at[1]),
        pltpu.make_async_copy(codes_hbm, codes_v, local_sem.at[2]),
        pltpu.make_async_copy(task_hbm, task_v, local_sem.at[3]),
    ]
    for load in loads:
        load.start()
    barrier = pltpu.get_barrier_semaphore()
    for step in NEIGHBOURS:
        pl.semaphore_signal(barrier, inc=1, device_id=device(step), device_id_type=MESH)

    loads[0].wait()
    loads[1].wait()
    act = act_v[...]
    start = start_v[...]
    row = (start >> 8) + HALO
    col = (start & 255) + HALO
    row += jnp.sum((act == 2).astype(I32) - (act == 1).astype(I32), axis=0, keepdims=True)
    col += jnp.sum((act == 4).astype(I32) - (act == 3).astype(I32), axis=0, keepdims=True)
    cells_v[...] = row * STRIDE + col

    loads[2].wait()
    lane = iota((64, LANES), 1)
    west = jnp.zeros((64, LANES), I32)
    east = jnp.zeros((64, LANES), I32)
    for q in range(4):
        mine = (lane >= 32 * q) & (lane < 32 * q + 32)
        rows = pl.ds(64 * q, 64)
        west = jnp.where(mine, pltpu.roll(codes_v[rows, 0:128], 32 * q, 1), west)
        east = jnp.where(mine, pltpu.roll(codes_v[rows, 128:256], (32 * q + 32) % 128, 1), east)
    w_send[...] = west
    e_send[...] = east
    pl.semaphore_wait(barrier, 8)
    copies = []

    def send(source, target, step):
        k = len(copies)
        copy = pltpu.make_async_remote_copy(
            source, target, send_sem.at[k], recv_sem.at[k],
            device_id=device(step), device_id_type=MESH,
        )
        copy.start()
        copies.append(copy)

    send(cells_v, side_out.at[1], (0, -1))
    send(cells_v, side_out.at[0], (0, 1))
    send(w_send, e_out, (0, -1))
    send(e_send, w_out, (0, 1))
    send(cells_v, lists_v.at[1], (-1, 0))
    send(cells_v, lists_v.at[0], (1, 0))
    send(codes_v.at[pl.ds(0, 32)], s_v, (-1, 0))
    send(codes_v.at[pl.ds(224, 32)], n_v, (1, 0))

    targets = [hot(inner_slots(col), 256), hot(slots(col, 0, FAR), 128), hot(slots(col, 16, 256), 128)]
    own = dot(hot(row, EXT), jnp.concatenate(targets, axis=0), NT)
    for c in range(2):
        count_v[c] = own[:, c * LANES : (c + 1) * LANES]
    edge_out[...] = own[:, 256:384]

    lane8 = iota((8, LANES), 1)
    lane24 = iota((24, LANES), 1)
    for k, (r, c) in enumerate(CORNERS):
        piece = jnp.zeros((8, LANES), I32)
        for q in range(4):
            mine = (lane8 >= 32 * q) & (lane8 < 32 * q + 32)
            rows = pl.ds((0 if r < 0 else 224) + 8 * q, 8)
            if c < 0:
                part = pltpu.roll(codes_v[rows, 0:128], 32 * q, 1)
            else:
                part = pltpu.roll(codes_v[rows, 128:256], (32 * q + 32) % 128, 1)
            piece = jnp.where(mine, part, piece)
        corner_send[k, 0:8, :] = piece
        first = 16 if r < 0 else 256
        upper = own[first : first + 24, 384:512]
        lower = own[first + 24 : first + 48, 384:512]
        if c < 0:
            lower = pltpu.roll(lower, 64, 1)
        else:
            upper = pltpu.roll(upper, 64, 1)
        corner_send[k, 8:32, :] = jnp.where(lane24 < 64, upper, lower).astype(I32)

    for k, step in enumerate(CORNERS):
        send(corner_send.at[k], corner_out.at[3 - k], step)

    loads[3].wait()
    block = (row * 1639) >> 16
    group = (col * 13108) >> 16
    task = task_v[...]
    place = (row - block * ROWS + 1) * BOTH + (task >> 1) * COLS + (col - group * COLS)
    place = place * 8 + block
    lane_of = (task & 1) * TASK_LANES + group
    for k in range(16):
        part = slice(k * LANES, (k + 1) * LANES)
        index_out[k : k + 1, :] = place[:, part]
        select_out[part, :] = jnp.broadcast_to(lane_of[:, part], (LANES, LANES)).T

    slot = iota((384, LANES), 0)
    code_col = jnp.where(slot < 256, slot + HALO, jnp.where(slot < 288, slot - 256, slot))
    code_col = jnp.where(slot < 320, code_col, -1)
    count_col = jnp.where(slot < FAR - EDGE, slot + EDGE, -1)
    count_col = jnp.where((slot >= 256) & (slot < 256 + EDGE), slot - 256, count_col)
    count_col = jnp.where((slot >= 320) & (slot < 320 + EDGE), slot - 320 + FAR, count_col)
    first_col = (iota((1, LANES), 1) & 63) * COLS
    in_lane = iota((LANES, LANES), 0)
    to_lane = iota((LANES, LANES), 1)
    for j in range(COLS):
        part = slice(j * LANES, (j + 1) * LANES)
        spread_codes[:, part] = one(code_col == first_col + j, BF16)
        spread_counts[:, part] = one(count_col == first_col + j, BF16)
        column = (in_lane & 63) * COLS + (j - HALO)
        column = jnp.where((column >= 0) & (column < TILE), column + (in_lane >> 6) * TILE, -1)
        for k in range(4):
            back_out[part, k * LANES : (k + 1) * LANES] = one(column == to_lane + k * LANES, BF16)

    for copy in copies[4:8]:
        copy.wait_recv()
    for k, first, step in ((0, 0, -1), (1, FAR, 1)):
        cells = lists_v[k]
        row = (cells >> 9) + step * TILE
        col = cells & (STRIDE - 1)
        targets = [hot(inner_slots(col), 256), hot(slots(col, 0, FAR), 128)]
        part = dot(hot(row - first, EDGE), jnp.concatenate(targets, axis=0), NT)
        band = slice(first, first + EDGE)
        for c in range(2):
            count_v[c, band, :] += part[:, c * LANES : (c + 1) * LANES]
        edge_out[band, :] += part[:, 256:384]
    for c in range(2):
        part = slice(c * LANES, (c + 1) * LANES)
        wide_v[c, 0:32, :] = n_v[:, part].astype(F32)
        wide_v[c, 32:288, :] = codes_v[:, part].astype(F32)
        wide_v[c, 288:320, :] = s_v[:, part].astype(F32)
    high, low = limbs(interleaved(count_v, 2))
    minus_out[...] = dot(high, spread_counts[0:256, :]) + dot(low, spread_counts[0:256, :])
    code_out[...] = dot(interleaved(wide_v, 2).astype(BF16), spread_codes[0:256, :])
    for k, copy in enumerate(copies):
        if not 4 <= k < 8:
            copy.wait_recv()
    for copy in copies:
        copy.wait_send()


def exchange(codes, start, actions, task):
    return pl.pallas_call(
        exchange_kernel,
        out_shape=(
            pltpu.VMEM((2, 1, AGENTS), I32),
            pltpu.VMEM((64, LANES), I32),
            pltpu.VMEM((64, LANES), I32),
            pltpu.VMEM((4, 32, LANES), I32),
            pltpu.VMEM((EXT, LANES), F32),
            pltpu.VMEM((EXT, WIDE), F32),
            pltpu.VMEM((EXT, WIDE), F32),
            pltpu.VMEM((384, WIDE), BF16),
            pltpu.VMEM((384, WIDE), BF16),
            pltpu.VMEM((WIDE, 2 * TILE), BF16),
            pltpu.VMEM((16, LANES), I32),
            pltpu.VMEM((AGENTS, LANES), I32),
        ),
        in_specs=[pl.BlockSpec(memory_space=pltpu.HBM)] * 4,
        out_specs=[pl.BlockSpec(memory_space=pltpu.VMEM)] * 12,
        scratch_shapes=[
            pltpu.VMEM((2, 1, AGENTS), I32),
            pltpu.VMEM((32, TILE), I32),
            pltpu.VMEM((32, TILE), I32),
            pltpu.VMEM((TILE, TILE), I32),
            pltpu.VMEM((2, EXT, LANES), F32),
            pltpu.VMEM((2, EXT, LANES), F32),
            pltpu.VMEM((1, AGENTS), I32),
            pltpu.VMEM((16, AGENTS), I32),
            pltpu.VMEM((1, AGENTS), I32),
            pltpu.VMEM((1, AGENTS), I32),
            pltpu.VMEM((64, LANES), I32),
            pltpu.VMEM((64, LANES), I32),
            pltpu.VMEM((4, 32, LANES), I32),
            pltpu.SemaphoreType.DMA((4,)),
            pltpu.SemaphoreType.DMA((12,)),
            pltpu.SemaphoreType.DMA((12,)),
        ],
        compiler_params=pltpu.CompilerParams(
            collective_id=0, has_side_effects=True, vmem_limit_bytes=24 << 20
        ),
        name="exchange",
    )(*[pltpu.with_memory_space_constraint(x, pltpu.HBM) for x in (start, actions, codes, task)])


def frame_kernel(
    lists_ref, w_ref, e_ref, corner_ref, own_ref, code_ref, minus_ref,
    spread_codes, spread_counts, back_ref, index_v, select_ref, table_hbm,
    values_out, agent_out,
    edge_v, reward_v, decay_v, val_a, val_b, natural_v, picked_v,
    index_s, table_ref, out_sem, index_sem, table_sem,
):
    to_smem = pltpu.make_async_copy(index_v, index_s, index_sem)
    to_smem.start()
    to_table = pltpu.make_async_copy(table_hbm, table_ref, table_sem)
    to_table.start()

    edges = own_ref[...]
    for k, step in ((0, -1), (1, 1)):
        cells = lists_ref[k]
        row = cells >> 9
        col = (cells & (STRIDE - 1)) + step * TILE
        edges += dot(hot(row, EXT), hot(slots(col, 0, FAR), 128), NT)
    edge_v[0] = edges
    lane24 = iota((24, LANES), 1)
    for first, pair_at in ((0, 0), (FAR, 2)):
        west = corner_ref[pair_at, 8:32, :].astype(F32)
        east = corner_ref[pair_at + 1, 8:32, :].astype(F32)
        west2 = pltpu.roll(west, 64, 1)
        east2 = pltpu.roll(east, 64, 1)
        edge_v[0, first : first + 24, :] += jnp.where(lane24 < 64, west, east2)
        edge_v[0, first + 24 : first + 48, :] += jnp.where(lane24 < 64, west2, east)

    lane = iota((64, LANES), 1)
    for q in range(4):
        west = pltpu.roll(w_ref[...], (128 - 32 * q) % 128, 1)
        east = pltpu.roll(e_ref[...], (160 - 32 * q) % 128, 1)
        both = jnp.where(lane < 32, west, jnp.where(lane < 64, east, 0))
        edge_v[1, 32 + 64 * q : 96 + 64 * q, :] = both.astype(F32)
        for first, pair_at in ((0, 0), (288, 2)):
            west = pltpu.roll(corner_ref[pair_at, 0:8, :], (128 - 32 * q) % 128, 1)
            east = pltpu.roll(corner_ref[pair_at + 1, 0:8, :], (160 - 32 * q) % 128, 1)
            both = jnp.where(lane[0:8] < 32, west, jnp.where(lane[0:8] < 64, east, 0))
            edge_v[1, first + 8 * q : first + 8 * q + 8, :] = both.astype(F32)

    last = interleaved(edge_v, 2)
    high, low = limbs(last[:, 0:LANES])
    spread = spread_counts[256:384, :]
    minus = dot(jnp.concatenate([high, low], axis=1), jnp.concatenate([spread, spread], axis=0))
    wide = dot(last[:, LANES:].astype(BF16), spread_codes[256:384, :])

    to_table.wait()
    lane8 = iota((8, LANES), 1)
    table = []
    for k in range(2):
        pair = jnp.concatenate([table_ref[2 * k : 2 * k + 1, :], table_ref[2 * k + 1 : 2 * k + 2, :]], axis=1)
        table.append(jnp.broadcast_to(pair, (8, LANES)))
    shift = (lane8 >> 6) * CODES
    for i in range(ROWS):
        for j in range(COLS):
            block = slice(8 * i, 8 * i + 8), slice(LANES * j, LANES * (j + 1))
            code = (wide[block] + code_ref[block]).astype(I32)
            at = code + shift
            less = minus[block] + minus_ref[block]
            decay_v[pl.ds((i * COLS + j) * 8, 8), :] = jnp.where(code < CODES - TERMINAL, GAMMA, 0.0)
            for p in range(2):
                reward = jnp.take_along_axis(table[p], at, axis=1) + less
                reward_v[pl.ds((i * BOTH + p * COLS + j) * 8, 8), :] = reward
                val_a[pl.ds(((i + 1) * BOTH + p * COLS + j) * 8, 8), :] = reward

    def take(ref, i):
        return [ref[pl.ds((i * BOTH + j) * 8, 8), :] for j in range(BOTH)]

    def put(ref, i, vregs):
        for j in range(BOTH):
            ref[pl.ds((i * BOTH + j) * 8, 8), :] = vregs[j]

    def wrap(ref):
        put(ref, 0, [pltpu.roll(x, 1, 0) for x in take(ref, ROWS)])
        put(ref, ROWS + 1, [pltpu.roll(x, 7, 0) for x in take(ref, 1)])

    def ends(row):
        first = [pltpu.roll(row[p], LANES - 1, 1) for p in (0, COLS)]
        last = [pltpu.roll(row[p + COLS - 1], 1, 1) for p in (0, COLS)]
        return first, last

    def pair(above, now, first):
        right = now[1:COLS] + [first[0]] + now[COLS + 1 :] + [first[1]]
        return [jnp.maximum(a, b) for a, b in zip(above, right)]

    def sweep(source, target):
        now = take(source, 1)
        first, last = ends(now)
        here = pair(take(source, 0), now, first)
        for i in range(ROWS):
            below = take(source, i + 2)
            first, next_last = ends(below)
            under = pair(now, below, first)
            new = [None] * BOTH
            for j in range(COLS):
                decay = decay_v[pl.ds((i * COLS + j) * 8, 8), :]
                for k, p in enumerate((0, COLS)):
                    other = under[p + j - 1] if j else jnp.maximum(last[k], below[p])
                    reward = reward_v[pl.ds((i * BOTH + p + j) * 8, 8), :]
                    new[p + j] = reward + decay * jnp.maximum(here[p + j], other)
            put(target, i + 1, new)
            now, here, last = below, under, next_last
        wrap(target)

    wrap(val_a)

    def two_sweeps(index, carry):
        sweep(val_a, val_b)
        sweep(val_b, val_a)
        return carry

    lax.fori_loop(0, SWEEPS // 2, two_sweeps, 0)

    back = back_ref[...]
    stores = []
    for p in range(2):
        parts = []
        for j in range(COLS):
            rows = [val_a[pl.ds(((i + 1) * BOTH + p * COLS + j) * 8, 8), :] for i in range(ROWS)]
            parts.append(jnp.concatenate(rows, axis=0))
        block = jnp.concatenate(parts, axis=1)
        upper = block.astype(BF16)
        lower = (block - upper.astype(F32)).astype(BF16)
        flat = dot(upper, back) + dot(lower, back)
        for c in range(4):
            for i in range(ROWS):
                piece = flat[8 * i : 8 * i + 8, c * LANES : (c + 1) * LANES]
                natural_v[4 * p + c, pl.ds(i, 8, stride=ROWS), :] = piece
            stores.append(
                pltpu.make_async_copy(
                    natural_v.at[4 * p + c, pl.ds(HALO, TILE)],
                    values_out.at[2 * p + c // 2, :, pl.ds(c % 2 * LANES, LANES)],
                    out_sem.at[4 * p + c],
                )
            )
            stores[-1].start()

    to_smem.wait()

    def pick(k, carry):
        for a in range(LANES):
            picked_v[pl.ds(k * LANES + a, 1), :] = val_a[pl.ds(index_s[k, a], 1), :]
        return carry

    lax.fori_loop(0, 16, pick, 0)
    diagonal = iota((LANES, LANES), 0) == iota((LANES, LANES), 1)
    for k in range(16):
        part = slice(k * LANES, (k + 1) * LANES)
        found = jnp.concatenate(
            [
                jnp.take_along_axis(
                    picked_v[k * LANES + 8 * a : k * LANES + 8 * a + 8, :],
                    select_ref[k * LANES + 8 * a : k * LANES + 8 * a + 8, :],
                    axis=1,
                )
                for a in range(16)
            ],
            axis=0,
        )
        agent_out[:, part] = jnp.sum(jnp.where(diagonal, found, 0.0), axis=0, keepdims=True)
    for store in stores:
        store.wait()


def frame(*arrays):
    return pl.pallas_call(
        frame_kernel,
        out_shape=(
            jax.ShapeDtypeStruct((4, TILE, TILE), F32),
            jax.ShapeDtypeStruct((1, AGENTS), F32),
        ),
        in_specs=[pl.BlockSpec(memory_space=pltpu.VMEM)] * 12 + [pl.BlockSpec(memory_space=pltpu.HBM)],
        out_specs=[pl.BlockSpec(memory_space=pltpu.HBM), pl.BlockSpec(memory_space=pltpu.VMEM)],
        scratch_shapes=[
            pltpu.VMEM((2, EXT, LANES), F32),
            pltpu.VMEM((ROWS * BOTH * 8, LANES), F32),
            pltpu.VMEM((ROWS * COLS * 8, LANES), F32),
            pltpu.VMEM(((ROWS + 2) * BOTH * 8, LANES), F32),
            pltpu.VMEM(((ROWS + 2) * BOTH * 8, LANES), F32),
            pltpu.VMEM((8, EXT, LANES), F32),
            pltpu.VMEM((AGENTS, LANES), F32),
            pltpu.SMEM((16, LANES), I32),
            pltpu.VMEM((4, CODES), F32),
            pltpu.SemaphoreType.DMA((8,)),
            pltpu.SemaphoreType.DMA,
            pltpu.SemaphoreType.DMA,
        ],
        compiler_params=pltpu.CompilerParams(vmem_limit_bytes=40 << 20),
        name="frame",
    )(*arrays)


def on_device(map_codes, reward_table, start_cell, agent_task, actions):
    arrived = exchange(
        map_codes, start_cell.reshape(1, AGENTS), actions, agent_task.reshape(1, AGENTS)
    )
    values, agent_value = frame(*arrived, pltpu.with_memory_space_constraint(reward_table, pltpu.HBM))
    return values, agent_value.reshape(AGENTS)


def solution(mesh):
    placed = (P("gy", "gx"), P(), P(("gx", "gy")), P(("gx", "gy")), P(None, ("gx", "gy")))
    return jax.shard_map(
        on_device,
        mesh=mesh,
        in_specs=placed,
        out_specs=(P(None, "gy", "gx"), P(("gx", "gy"))),
        check_vma=False,
    )
```

```python
import functools

import jax
import jax.numpy as jnp
from jax import lax
from jax.experimental import pallas as pl
from jax.experimental.pallas import tpu as pltpu
from jax.sharding import PartitionSpec as P

SWEEPS = 16
CODES = 64
TERMINAL = 2
GAMMA = 0.95
PENALTY = 0.5
CORNERS = ((-1, -1), (-1, 1), (1, -1), (1, 1))
SIDES = ((-1, 0), (0, -1), (0, 1), (1, 0))
NEIGHBOURS = ((-1, -1), (-1, 0), (-1, 1), (0, -1), (0, 1), (1, -1), (1, 0), (1, 1))

TILE = 256
HALO = 32
EXT = TILE + 2 * HALO
ROWS = EXT // 8
COLS = 5
LANES = 128
TASK_LANES = 64
WIDE = COLS * LANES
BOTH = 2 * COLS
AGENTS = 2048
STRIDE = 512
EDGE = 48
FAR = EXT - EDGE

F32 = jnp.float32
BF16 = jnp.bfloat16
F8 = jnp.float8_e4m3fn
I32 = jnp.int32
MESH = pl.DeviceIdType.MESH
NT = (((1,), (1,)), ((), ()))
NN = (((1,), (0,)), ((), ()))


def dot(a, b, dims=NN):
    return lax.dot_general(a, b, dims, preferred_element_type=F32)


def iota(shape, dim):
    return lax.broadcasted_iota(I32, shape, dim)


def one(match, kind):
    return jnp.where(match, 1.0, 0.0).astype(kind)


def hot(values, count):
    return one(iota((count, values.shape[1]), 0) == values, F8)


def slots(cols, low, high):
    near = (cols >= low) & (cols < low + EDGE)
    far = (cols >= high) & (cols < high + EDGE)
    return jnp.where(near, cols - low, jnp.where(far, cols - high + 64, -1))


def inner_slots(cols):
    return jnp.where((cols >= EDGE) & (cols < FAR), cols - EDGE, -1)


def interleaved(ref, tiles):
    parts = []
    for c in range(tiles):
        rows = [ref[c, pl.ds(i, 8, stride=ROWS), :] for i in range(ROWS)]
        parts.append(jnp.concatenate(rows, axis=0))
    return jnp.concatenate(parts, axis=1)


def limbs(counts):
    high = jnp.floor(counts * (1.0 / 128.0))
    low = counts - high * 128.0
    return (high * (-128.0 * PENALTY)).astype(BF16), (low * -PENALTY).astype(BF16)


def exchange_kernel(
    start_hbm, act_hbm, codes_hbm, task_hbm,
    w_out, e_out, corner_out, edge_out, code_out, minus_out,
    spread_codes, spread_counts, back_out, index_out, select_out,
    lists_v, n_v, s_v, codes_v, count_v, wide_v, start_v, act_v, task_v, cells_v, w_send, e_send, corner_send, local_sem, send_sem, recv_sem,
):
    gx = lax.axis_index("gx")
    gy = lax.axis_index("gy")

    def device(step):
        return (lax.rem(gx + step[1] + 16, 16), lax.rem(gy + step[0] + 16, 16))

    loads = [
        pltpu.make_async_copy(act_hbm, act_v, local_sem.at[0]),
        pltpu.make_async_copy(start_hbm, start_v, local_sem.at[1]),
        pltpu.make_async_copy(codes_hbm, codes_v, local_sem.at[2]),
        pltpu.make_async_copy(task_hbm, task_v, local_sem.at[3]),
    ]
    for load in loads:
        load.start()
    barrier = pltpu.get_barrier_semaphore()
    for step in NEIGHBOURS:
        pl.semaphore_signal(barrier, inc=1, device_id=device(step), device_id_type=MESH)

    loads[0].wait()
    loads[1].wait()
    act = act_v[...]
    start = start_v[...]
    row = (start >> 8) + HALO
    col = (start & 255) + HALO
    row += jnp.sum((act == 2).astype(I32) - (act == 1).astype(I32), axis=0, keepdims=True)
    col += jnp.sum((act == 4).astype(I32) - (act == 3).astype(I32), axis=0, keepdims=True)
    cells_v[...] = row * STRIDE + col

    loads[2].wait()
    lane = iota((64, LANES), 1)
    west = jnp.zeros((64, LANES), I32)
    east = jnp.zeros((64, LANES), I32)
    for q in range(4):
        mine = (lane >= 32 * q) & (lane < 32 * q + 32)
        rows = pl.ds(64 * q, 64)
        west = jnp.where(mine, pltpu.roll(codes_v[rows, 0:128], 32 * q, 1), west)
        east = jnp.where(mine, pltpu.roll(codes_v[rows, 128:256], (32 * q + 32) % 128, 1), east)
    w_send[...] = west
    e_send[...] = east
    pl.semaphore_wait(barrier, 8)
    copies = []

    def send(source, target, step):
        k = len(copies)
        copy = pltpu.make_async_remote_copy(
            source, target, send_sem.at[k], recv_sem.at[k],
            device_id=device(step), device_id_type=MESH,
        )
        copy.start()
        copies.append(copy)

    send(cells_v, lists_v.at[3], (0, -1))
    send(cells_v, lists_v.at[2], (0, 1))
    send(w_send, e_out, (0, -1))
    send(e_send, w_out, (0, 1))
    send(cells_v, lists_v.at[1], (-1, 0))
    send(cells_v, lists_v.at[0], (1, 0))
    send(codes_v.at[pl.ds(0, 32)], s_v, (-1, 0))
    send(codes_v.at[pl.ds(224, 32)], n_v, (1, 0))

    targets = [hot(inner_slots(col), 256), hot(slots(col, 0, FAR), 128), hot(slots(col, 16, 256), 128)]
    own = dot(hot(row, EXT), jnp.concatenate(targets, axis=0), NT)
    for c in range(2):
        count_v[c] = own[:, c * LANES : (c + 1) * LANES]
    edge_out[...] = own[:, 256:384]

    lane8 = iota((8, LANES), 1)
    lane24 = iota((24, LANES), 1)
    for k, (r, c) in enumerate(CORNERS):
        piece = jnp.zeros((8, LANES), I32)
        for q in range(4):
            mine = (lane8 >= 32 * q) & (lane8 < 32 * q + 32)
            rows = pl.ds((0 if r < 0 else 224) + 8 * q, 8)
            if c < 0:
                part = pltpu.roll(codes_v[rows, 0:128], 32 * q, 1)
            else:
                part = pltpu.roll(codes_v[rows, 128:256], (32 * q + 32) % 128, 1)
            piece = jnp.where(mine, part, piece)
        corner_send[k, 0:8, :] = piece
        first = 16 if r < 0 else 256
        upper = own[first : first + 24, 384:512]
        lower = own[first + 24 : first + 48, 384:512]
        if c < 0:
            lower = pltpu.roll(lower, 64, 1)
        else:
            upper = pltpu.roll(upper, 64, 1)
        corner_send[k, 8:32, :] = jnp.where(lane24 < 64, upper, lower).astype(I32)

    for k, step in enumerate(CORNERS):
        send(corner_send.at[k], corner_out.at[3 - k], step)

    loads[3].wait()
    block = (row * 1639) >> 16
    group = (col * 13108) >> 16
    task = task_v[...]
    place = (row - block * ROWS + 1) * BOTH + (task >> 1) * COLS + (col - group * COLS)
    place = place * 8 + block
    lane_of = (task & 1) * TASK_LANES + group
    for k in range(16):
        part = slice(k * LANES, (k + 1) * LANES)
        index_out[k : k + 1, :] = place[:, part]
        select_out[part, :] = jnp.broadcast_to(lane_of[:, part], (LANES, LANES)).T

    slot = iota((384, LANES), 0)
    code_col = jnp.where(slot < 256, slot + HALO, jnp.where(slot < 288, slot - 256, slot))
    code_col = jnp.where(slot < 320, code_col, -1)
    count_col = jnp.where(slot < FAR - EDGE, slot + EDGE, -1)
    count_col = jnp.where((slot >= 256) & (slot < 256 + EDGE), slot - 256, count_col)
    count_col = jnp.where((slot >= 320) & (slot < 320 + EDGE), slot - 320 + FAR, count_col)
    first_col = (iota((1, LANES), 1) & 63) * COLS
    in_lane = iota((LANES, LANES), 0)
    to_lane = iota((LANES, LANES), 1)
    for j in range(COLS):
        part = slice(j * LANES, (j + 1) * LANES)
        spread_codes[:, part] = one(code_col == first_col + j, BF16)
        spread_counts[:, part] = one(count_col == first_col + j, BF16)
        column = (in_lane & 63) * COLS + (j - HALO)
        column = jnp.where((column >= 0) & (column < TILE), column + (in_lane >> 6) * TILE, -1)
        for k in range(4):
            back_out[part, k * LANES : (k + 1) * LANES] = one(column == to_lane + k * LANES, BF16)

    for copy in copies[4:8]:
        copy.wait_recv()
    for k, first, step in ((0, 0, -1), (1, FAR, 1)):
        cells = lists_v[k]
        row = (cells >> 9) + step * TILE
        col = cells & (STRIDE - 1)
        targets = [hot(inner_slots(col), 256), hot(slots(col, 0, FAR), 128)]
        part = dot(hot(row - first, EDGE), jnp.concatenate(targets, axis=0), NT)
        band = slice(first, first + EDGE)
        for c in range(2):
            count_v[c, band, :] += part[:, c * LANES : (c + 1) * LANES]
        edge_out[band, :] += part[:, 256:384]
    for c in range(2):
        part = slice(c * LANES, (c + 1) * LANES)
        wide_v[c, 0:32, :] = n_v[:, part].astype(F32)
        wide_v[c, 32:288, :] = codes_v[:, part].astype(F32)
        wide_v[c, 288:320, :] = s_v[:, part].astype(F32)
    high, low = limbs(interleaved(count_v, 2))
    minus_out[...] = dot(high, spread_counts[0:256, :]) + dot(low, spread_counts[0:256, :])
    code_out[...] = dot(interleaved(wide_v, 2).astype(BF16), spread_codes[0:256, :])
    for k, step in ((0, 1), (1, -1)):
        copies[k].wait_recv()
        cells = lists_v[3 - k]
        col = (cells & (STRIDE - 1)) + step * TILE
        edge_out[...] += dot(hot(cells >> 9, EXT), hot(slots(col, 0, FAR), 128), NT)
    for k, copy in enumerate(copies):
        if k in (2, 3) or k >= 8:
            copy.wait_recv()
    for copy in copies:
        copy.wait_send()


def exchange(codes, start, actions, task):
    return pl.pallas_call(
        exchange_kernel,
        out_shape=(
            pltpu.VMEM((64, LANES), I32),
            pltpu.VMEM((64, LANES), I32),
            pltpu.VMEM((4, 32, LANES), I32),
            pltpu.VMEM((EXT, LANES), F32),
            pltpu.VMEM((EXT, WIDE), F32),
            pltpu.VMEM((EXT, WIDE), F32),
            pltpu.VMEM((384, WIDE), BF16),
            pltpu.VMEM((384, WIDE), BF16),
            pltpu.VMEM((WIDE, 2 * TILE), BF16),
            pltpu.VMEM((16, LANES), I32),
            pltpu.VMEM((AGENTS, LANES), I32),
        ),
        in_specs=[pl.BlockSpec(memory_space=pltpu.HBM)] * 4,
        out_specs=[pl.BlockSpec(memory_space=pltpu.VMEM)] * 11,
        scratch_shapes=[
            pltpu.VMEM((4, 1, AGENTS), I32),
            pltpu.VMEM((32, TILE), I32),
            pltpu.VMEM((32, TILE), I32),
            pltpu.VMEM((TILE, TILE), I32),
            pltpu.VMEM((2, EXT, LANES), F32),
            pltpu.VMEM((2, EXT, LANES), F32),
            pltpu.VMEM((1, AGENTS), I32),
            pltpu.VMEM((16, AGENTS), I32),
            pltpu.VMEM((1, AGENTS), I32),
            pltpu.VMEM((1, AGENTS), I32),
            pltpu.VMEM((64, LANES), I32),
            pltpu.VMEM((64, LANES), I32),
            pltpu.VMEM((4, 32, LANES), I32),
            pltpu.SemaphoreType.DMA((4,)),
            pltpu.SemaphoreType.DMA((12,)),
            pltpu.SemaphoreType.DMA((12,)),
        ],
        compiler_params=pltpu.CompilerParams(
            collective_id=0, has_side_effects=True, vmem_limit_bytes=24 << 20
        ),
        name="exchange",
    )(*[pltpu.with_memory_space_constraint(x, pltpu.HBM) for x in (start, actions, codes, task)])


def frame_kernel(
    w_ref, e_ref, corner_ref, own_ref, code_ref, minus_ref,
    spread_codes, spread_counts, back_ref, index_v, select_ref, table_hbm,
    values_out, agent_out,
    edge_v, reward_v, decay_v, val_a, val_b, natural_v, picked_v,
    index_s, table_ref, out_sem, index_sem, table_sem,
):
    to_smem = pltpu.make_async_copy(index_v, index_s, index_sem)
    to_smem.start()
    to_table = pltpu.make_async_copy(table_hbm, table_ref, table_sem)
    to_table.start()

    edge_v[0] = own_ref[...]
    lane24 = iota((24, LANES), 1)
    for first, pair_at in ((0, 0), (FAR, 2)):
        west = corner_ref[pair_at, 8:32, :].astype(F32)
        east = corner_ref[pair_at + 1, 8:32, :].astype(F32)
        west2 = pltpu.roll(west, 64, 1)
        east2 = pltpu.roll(east, 64, 1)
        edge_v[0, first : first + 24, :] += jnp.where(lane24 < 64, west, east2)
        edge_v[0, first + 24 : first + 48, :] += jnp.where(lane24 < 64, west2, east)

    lane = iota((64, LANES), 1)
    for q in range(4):
        west = pltpu.roll(w_ref[...], (128 - 32 * q) % 128, 1)
        east = pltpu.roll(e_ref[...], (160 - 32 * q) % 128, 1)
        both = jnp.where(lane < 32, west, jnp.where(lane < 64, east, 0))
        edge_v[1, 32 + 64 * q : 96 + 64 * q, :] = both.astype(F32)
        for first, pair_at in ((0, 0), (288, 2)):
            west = pltpu.roll(corner_ref[pair_at, 0:8, :], (128 - 32 * q) % 128, 1)
            east = pltpu.roll(corner_ref[pair_at + 1, 0:8, :], (160 - 32 * q) % 128, 1)
            both = jnp.where(lane[0:8] < 32, west, jnp.where(lane[0:8] < 64, east, 0))
            edge_v[1, first + 8 * q : first + 8 * q + 8, :] = both.astype(F32)

    last = interleaved(edge_v, 2)
    high, low = limbs(last[:, 0:LANES])
    spread = spread_counts[256:384, :]
    minus = dot(jnp.concatenate([high, low], axis=1), jnp.concatenate([spread, spread], axis=0))
    wide = dot(last[:, LANES:].astype(BF16), spread_codes[256:384, :])

    to_table.wait()
    lane8 = iota((8, LANES), 1)
    table = []
    for k in range(2):
        pair = jnp.concatenate([table_ref[2 * k : 2 * k + 1, :], table_ref[2 * k + 1 : 2 * k + 2, :]], axis=1)
        table.append(jnp.broadcast_to(pair, (8, LANES)))
    shift = (lane8 >> 6) * CODES
    for i in range(ROWS):
        for j in range(COLS):
            block = slice(8 * i, 8 * i + 8), slice(LANES * j, LANES * (j + 1))
            code = (wide[block] + code_ref[block]).astype(I32)
            at = code + shift
            less = minus[block] + minus_ref[block]
            decay_v[pl.ds((i * COLS + j) * 8, 8), :] = jnp.where(code < CODES - TERMINAL, GAMMA, 0.0)
            for p in range(2):
                reward = jnp.take_along_axis(table[p], at, axis=1) + less
                reward_v[pl.ds((i * BOTH + p * COLS + j) * 8, 8), :] = reward
                val_a[pl.ds(((i + 1) * BOTH + p * COLS + j) * 8, 8), :] = reward

    def take(ref, i):
        return [ref[pl.ds((i * BOTH + j) * 8, 8), :] for j in range(BOTH)]

    def put(ref, i, vregs):
        for j in range(BOTH):
            ref[pl.ds((i * BOTH + j) * 8, 8), :] = vregs[j]

    def wrap(ref):
        put(ref, 0, [pltpu.roll(x, 1, 0) for x in take(ref, ROWS)])
        put(ref, ROWS + 1, [pltpu.roll(x, 7, 0) for x in take(ref, 1)])

    def ends(row):
        first = [pltpu.roll(row[p], LANES - 1, 1) for p in (0, COLS)]
        last = [pltpu.roll(row[p + COLS - 1], 1, 1) for p in (0, COLS)]
        return first, last

    def pair(above, now, first):
        right = now[1:COLS] + [first[0]] + now[COLS + 1 :] + [first[1]]
        return [jnp.maximum(a, b) for a, b in zip(above, right)]

    def sweep(source, target):
        now = take(source, 1)
        first, last = ends(now)
        here = pair(take(source, 0), now, first)
        for i in range(ROWS):
            below = take(source, i + 2)
            first, next_last = ends(below)
            under = pair(now, below, first)
            new = [None] * BOTH
            for j in range(COLS):
                decay = decay_v[pl.ds((i * COLS + j) * 8, 8), :]
                for k, p in enumerate((0, COLS)):
                    other = under[p + j - 1] if j else jnp.maximum(last[k], below[p])
                    reward = reward_v[pl.ds((i * BOTH + p + j) * 8, 8), :]
                    new[p + j] = reward + decay * jnp.maximum(here[p + j], other)
            put(target, i + 1, new)
            now, here, last = below, under, next_last
        wrap(target)

    wrap(val_a)

    def two_sweeps(index, carry):
        sweep(val_a, val_b)
        sweep(val_b, val_a)
        return carry

    lax.fori_loop(0, SWEEPS // 2, two_sweeps, 0)

    to_smem.wait()
    for k in range(16):
        for a in range(LANES):
            picked_v[pl.ds(k * LANES + a, 1), :] = val_a[pl.ds(index_s[k, a], 1), :]

    back = back_ref[...]
    stores = []
    for p in range(2):
        parts = []
        for j in range(COLS):
            rows = [val_a[pl.ds(((i + 1) * BOTH + p * COLS + j) * 8, 8), :] for i in range(ROWS)]
            parts.append(jnp.concatenate(rows, axis=0))
        block = jnp.concatenate(parts, axis=1)
        upper = block.astype(BF16)
        lower = (block - upper.astype(F32)).astype(BF16)
        flat = dot(upper, back) + dot(lower, back)
        for c in range(4):
            for i in range(ROWS):
                piece = flat[8 * i : 8 * i + 8, c * LANES : (c + 1) * LANES]
                natural_v[4 * p + c, pl.ds(i, 8, stride=ROWS), :] = piece
            stores.append(
                pltpu.make_async_copy(
                    natural_v.at[4 * p + c, pl.ds(HALO, TILE)],
                    values_out.at[2 * p + c // 2, :, pl.ds(c % 2 * LANES, LANES)],
                    out_sem.at[4 * p + c],
                )
            )
            stores[-1].start()

    diagonal = iota((LANES, LANES), 0) == iota((LANES, LANES), 1)
    for k in range(16):
        part = slice(k * LANES, (k + 1) * LANES)
        found = jnp.concatenate(
            [
                jnp.take_along_axis(
                    picked_v[k * LANES + 8 * a : k * LANES + 8 * a + 8, :],
                    select_ref[k * LANES + 8 * a : k * LANES + 8 * a + 8, :],
                    axis=1,
                )
                for a in range(16)
            ],
            axis=0,
        )
        agent_out[:, part] = jnp.sum(jnp.where(diagonal, found, 0.0), axis=0, keepdims=True)
    for store in stores:
        store.wait()


def frame(*arrays):
    return pl.pallas_call(
        frame_kernel,
        out_shape=(
            jax.ShapeDtypeStruct((4, TILE, TILE), F32),
            jax.ShapeDtypeStruct((1, AGENTS), F32),
        ),
        in_specs=[pl.BlockSpec(memory_space=pltpu.VMEM)] * 11 + [pl.BlockSpec(memory_space=pltpu.HBM)],
        out_specs=[pl.BlockSpec(memory_space=pltpu.HBM), pl.BlockSpec(memory_space=pltpu.VMEM)],
        scratch_shapes=[
            pltpu.VMEM((2, EXT, LANES), F32),
            pltpu.VMEM((ROWS * BOTH * 8, LANES), F32),
            pltpu.VMEM((ROWS * COLS * 8, LANES), F32),
            pltpu.VMEM(((ROWS + 2) * BOTH * 8, LANES), F32),
            pltpu.VMEM(((ROWS + 2) * BOTH * 8, LANES), F32),
            pltpu.VMEM((8, EXT, LANES), F32),
            pltpu.VMEM((AGENTS, LANES), F32),
            pltpu.SMEM((16, LANES), I32),
            pltpu.VMEM((4, CODES), F32),
            pltpu.SemaphoreType.DMA((8,)),
            pltpu.SemaphoreType.DMA,
            pltpu.SemaphoreType.DMA,
        ],
        compiler_params=pltpu.CompilerParams(vmem_limit_bytes=40 << 20),
        name="frame",
    )(*arrays)


def on_device(map_codes, reward_table, start_cell, agent_task, actions):
    arrived = exchange(
        map_codes, start_cell.reshape(1, AGENTS), actions, agent_task.reshape(1, AGENTS)
    )
    values, agent_value = frame(*arrived, pltpu.with_memory_space_constraint(reward_table, pltpu.HBM))
    return values, agent_value.reshape(AGENTS)


def solution(mesh):
    placed = (P("gy", "gx"), P(), P(("gx", "gy")), P(("gx", "gy")), P(None, ("gx", "gy")))
    return jax.shard_map(
        on_device,
        mesh=mesh,
        in_specs=placed,
        out_specs=(P(None, "gy", "gx"), P(("gx", "gy"))),
        check_vma=False,
    )
```

```python
import functools

import jax
import jax.numpy as jnp
from jax import lax
from jax.experimental import pallas as pl
from jax.experimental.pallas import tpu as pltpu
from jax.sharding import PartitionSpec as P

SWEEPS = 16
CODES = 64
TERMINAL = 2
GAMMA = 0.95
PENALTY = 0.5
CORNERS = ((-1, -1), (-1, 1), (1, -1), (1, 1))
SIDES = ((-1, 0), (0, -1), (0, 1), (1, 0))
NEIGHBOURS = ((-1, -1), (-1, 0), (-1, 1), (0, -1), (0, 1), (1, -1), (1, 0), (1, 1))

TILE = 256
HALO = 32
EXT = TILE + 2 * HALO
ROWS = EXT // 8
COLS = 5
LANES = 128
TASK_LANES = 64
WIDE = COLS * LANES
BOTH = 2 * COLS
AGENTS = 2048
STRIDE = 512
EDGE = 48
FAR = EXT - EDGE

F32 = jnp.float32
BF16 = jnp.bfloat16
F8 = jnp.float8_e4m3fn
I32 = jnp.int32
MESH = pl.DeviceIdType.MESH
NT = (((1,), (1,)), ((), ()))
NN = (((1,), (0,)), ((), ()))


def dot(a, b, dims=NN):
    return lax.dot_general(a, b, dims, preferred_element_type=F32)


def iota(shape, dim):
    return lax.broadcasted_iota(I32, shape, dim)


def one(match, kind):
    return jnp.where(match, 1.0, 0.0).astype(kind)


def hot(values, count):
    return one(iota((count, values.shape[1]), 0) == values, F8)


def slots(cols, low, high):
    near = (cols >= low) & (cols < low + EDGE)
    far = (cols >= high) & (cols < high + EDGE)
    return jnp.where(near, cols - low, jnp.where(far, cols - high + 64, -1))


def inner_slots(cols):
    return jnp.where((cols >= EDGE) & (cols < FAR), cols - EDGE, -1)


def interleaved(ref, tiles):
    parts = []
    for c in range(tiles):
        rows = [ref[c, pl.ds(i, 8, stride=ROWS), :] for i in range(ROWS)]
        parts.append(jnp.concatenate(rows, axis=0))
    return jnp.concatenate(parts, axis=1)


def limbs(counts):
    high = jnp.floor(counts * (1.0 / 128.0))
    low = counts - high * 128.0
    return (high * (-128.0 * PENALTY)).astype(BF16), (low * -PENALTY).astype(BF16)


def exchange_kernel(
    start_hbm, act_hbm, codes_hbm, task_hbm,
    w_out, e_out, corner_out, edge_out, code_out, minus_out,
    spread_codes, spread_counts, back_out, index_out, select_out,
    lists_v, n_v, s_v, codes_v, count_v, wide_v, start_v, act_v, task_v, cells_v, w_send, e_send, corner_send, local_sem, send_sem, recv_sem,
):
    gx = lax.axis_index("gx")
    gy = lax.axis_index("gy")

    def device(step):
        return (lax.rem(gx + step[1] + 16, 16), lax.rem(gy + step[0] + 16, 16))

    loads = [
        pltpu.make_async_copy(act_hbm, act_v, local_sem.at[0]),
        pltpu.make_async_copy(start_hbm, start_v, local_sem.at[1]),
        pltpu.make_async_copy(codes_hbm, codes_v, local_sem.at[2]),
        pltpu.make_async_copy(task_hbm, task_v, local_sem.at[3]),
    ]
    for load in loads:
        load.start()
    barrier = pltpu.get_barrier_semaphore()
    for step in NEIGHBOURS:
        pl.semaphore_signal(barrier, inc=1, device_id=device(step), device_id_type=MESH)

    slot = iota((384, LANES), 0)
    code_col = jnp.where(slot < 256, slot + HALO, jnp.where(slot < 288, slot - 256, slot))
    code_col = jnp.where(slot < 320, code_col, -1)
    count_col = jnp.where(slot < FAR - EDGE, slot + EDGE, -1)
    count_col = jnp.where((slot >= 256) & (slot < 256 + EDGE), slot - 256, count_col)
    count_col = jnp.where((slot >= 320) & (slot < 320 + EDGE), slot - 320 + FAR, count_col)
    first_col = (iota((1, LANES), 1) & 63) * COLS
    in_lane = iota((LANES, LANES), 0)
    to_lane = iota((LANES, LANES), 1)
    for j in range(COLS):
        part = slice(j * LANES, (j + 1) * LANES)
        spread_codes[:, part] = one(code_col == first_col + j, BF16)
        spread_counts[:, part] = one(count_col == first_col + j, BF16)
        column = (in_lane & 63) * COLS + (j - HALO)
        column = jnp.where((column >= 0) & (column < TILE), column + (in_lane >> 6) * TILE, -1)
        for k in range(4):
            back_out[part, k * LANES : (k + 1) * LANES] = one(column == to_lane + k * LANES, BF16)

    loads[0].wait()
    loads[1].wait()
    act = act_v[...]
    start = start_v[...]
    row = (start >> 8) + HALO
    col = (start & 255) + HALO
    row += jnp.sum((act == 2).astype(I32) - (act == 1).astype(I32), axis=0, keepdims=True)
    col += jnp.sum((act == 4).astype(I32) - (act == 3).astype(I32), axis=0, keepdims=True)
    cells_v[...] = row * STRIDE + col

    targets = [hot(inner_slots(col), 256), hot(slots(col, 0, FAR), 128), hot(slots(col, 16, 256), 128)]
    own = dot(hot(row, EXT), jnp.concatenate(targets, axis=0), NT)
    for c in range(2):
        count_v[c] = own[:, c * LANES : (c + 1) * LANES]
    edge_out[...] = own[:, 256:384]

    loads[2].wait()
    lane = iota((64, LANES), 1)
    west = jnp.zeros((64, LANES), I32)
    east = jnp.zeros((64, LANES), I32)
    for q in range(4):
        mine = (lane >= 32 * q) & (lane < 32 * q + 32)
        rows = pl.ds(64 * q, 64)
        west = jnp.where(mine, pltpu.roll(codes_v[rows, 0:128], 32 * q, 1), west)
        east = jnp.where(mine, pltpu.roll(codes_v[rows, 128:256], (32 * q + 32) % 128, 1), east)
    w_send[...] = west
    e_send[...] = east
    lane8 = iota((8, LANES), 1)
    lane24 = iota((24, LANES), 1)
    for k, (r, c) in enumerate(CORNERS):
        piece = jnp.zeros((8, LANES), I32)
        for q in range(4):
            mine = (lane8 >= 32 * q) & (lane8 < 32 * q + 32)
            rows = pl.ds((0 if r < 0 else 224) + 8 * q, 8)
            if c < 0:
                part = pltpu.roll(codes_v[rows, 0:128], 32 * q, 1)
            else:
                part = pltpu.roll(codes_v[rows, 128:256], (32 * q + 32) % 128, 1)
            piece = jnp.where(mine, part, piece)
        corner_send[k, 0:8, :] = piece
        first = 16 if r < 0 else 256
        upper = own[first : first + 24, 384:512]
        lower = own[first + 24 : first + 48, 384:512]
        if c < 0:
            lower = pltpu.roll(lower, 64, 1)
        else:
            upper = pltpu.roll(upper, 64, 1)
        corner_send[k, 8:32, :] = jnp.where(lane24 < 64, upper, lower).astype(I32)

    pl.semaphore_wait(barrier, 8)
    copies = []

    def send(source, target, step):
        k = len(copies)
        copy = pltpu.make_async_remote_copy(
            source, target, send_sem.at[k], recv_sem.at[k],
            device_id=device(step), device_id_type=MESH,
        )
        copy.start()
        copies.append(copy)

    send(cells_v, lists_v.at[1], (-1, 0))
    send(cells_v, lists_v.at[0], (1, 0))
    send(codes_v.at[pl.ds(0, 32)], s_v, (-1, 0))
    send(codes_v.at[pl.ds(224, 32)], n_v, (1, 0))
    send(cells_v, lists_v.at[3], (0, -1))
    send(cells_v, lists_v.at[2], (0, 1))
    for k, step in enumerate(CORNERS):
        send(corner_send.at[k], corner_out.at[3 - k], step)
    send(w_send, e_out, (0, -1))
    send(e_send, w_out, (0, 1))

    loads[3].wait()
    block = (row * 1639) >> 16
    group = (col * 13108) >> 16
    task = task_v[...]
    place = (row - block * ROWS + 1) * BOTH + (task >> 1) * COLS + (col - group * COLS)
    place = place * 8 + block
    lane_of = (task & 1) * TASK_LANES + group
    for k in range(16):
        part = slice(k * LANES, (k + 1) * LANES)
        index_out[k : k + 1, :] = place[:, part]
        select_out[part, :] = jnp.broadcast_to(lane_of[:, part], (LANES, LANES)).T

    for copy in copies[0:2] + copies[2:4]:
        copy.wait_recv()
    for k, first, step in ((0, 0, -1), (1, FAR, 1)):
        cells = lists_v[k]
        row = (cells >> 9) + step * TILE
        col = cells & (STRIDE - 1)
        targets = [hot(inner_slots(col), 256), hot(slots(col, 0, FAR), 128)]
        part = dot(hot(row - first, EDGE), jnp.concatenate(targets, axis=0), NT)
        band = slice(first, first + EDGE)
        for c in range(2):
            count_v[c, band, :] += part[:, c * LANES : (c + 1) * LANES]
        edge_out[band, :] += part[:, 256:384]
    for c in range(2):
        part = slice(c * LANES, (c + 1) * LANES)
        wide_v[c, 0:32, :] = n_v[:, part].astype(F32)
        wide_v[c, 32:288, :] = codes_v[:, part].astype(F32)
        wide_v[c, 288:320, :] = s_v[:, part].astype(F32)
    high, low = limbs(interleaved(count_v, 2))
    minus_out[...] = dot(high, spread_counts[0:256, :]) + dot(low, spread_counts[0:256, :])
    code_out[...] = dot(interleaved(wide_v, 2).astype(BF16), spread_codes[0:256, :])
    for k, step in ((0, 1), (1, -1)):
        copies[4 + k].wait_recv()
        cells = lists_v[3 - k]
        col = (cells & (STRIDE - 1)) + step * TILE
        edge_out[...] += dot(hot(cells >> 9, EXT), hot(slots(col, 0, FAR), 128), NT)
    for copy in copies[6:10] + copies[10:12]:
        copy.wait_recv()
    for copy in copies:
        copy.wait_send()


def exchange(codes, start, actions, task):
    return pl.pallas_call(
        exchange_kernel,
        out_shape=(
            pltpu.VMEM((64, LANES), I32),
            pltpu.VMEM((64, LANES), I32),
            pltpu.VMEM((4, 32, LANES), I32),
            pltpu.VMEM((EXT, LANES), F32),
            pltpu.VMEM((EXT, WIDE), F32),
            pltpu.VMEM((EXT, WIDE), F32),
            pltpu.VMEM((384, WIDE), BF16),
            pltpu.VMEM((384, WIDE), BF16),
            pltpu.VMEM((WIDE, 2 * TILE), BF16),
            pltpu.VMEM((16, LANES), I32),
            pltpu.VMEM((AGENTS, LANES), I32),
        ),
        in_specs=[pl.BlockSpec(memory_space=pltpu.HBM)] * 4,
        out_specs=[pl.BlockSpec(memory_space=pltpu.VMEM)] * 11,
        scratch_shapes=[
            pltpu.VMEM((4, 1, AGENTS), I32),
            pltpu.VMEM((32, TILE), I32),
            pltpu.VMEM((32, TILE), I32),
            pltpu.VMEM((TILE, TILE), I32),
            pltpu.VMEM((2, EXT, LANES), F32),
            pltpu.VMEM((2, EXT, LANES), F32),
            pltpu.VMEM((1, AGENTS), I32),
            pltpu.VMEM((16, AGENTS), I32),
            pltpu.VMEM((1, AGENTS), I32),
            pltpu.VMEM((1, AGENTS), I32),
            pltpu.VMEM((64, LANES), I32),
            pltpu.VMEM((64, LANES), I32),
            pltpu.VMEM((4, 32, LANES), I32),
            pltpu.SemaphoreType.DMA((4,)),
            pltpu.SemaphoreType.DMA((12,)),
            pltpu.SemaphoreType.DMA((12,)),
        ],
        compiler_params=pltpu.CompilerParams(
            collective_id=0, has_side_effects=True, vmem_limit_bytes=24 << 20
        ),
        name="exchange",
    )(*[pltpu.with_memory_space_constraint(x, pltpu.HBM) for x in (start, actions, codes, task)])


def frame_kernel(
    w_ref, e_ref, corner_ref, own_ref, code_ref, minus_ref,
    spread_codes, spread_counts, back_ref, index_v, select_ref, table_hbm,
    values_out, agent_out,
    edge_v, reward_v, decay_v, val_a, val_b, natural_v, picked_v,
    index_s, table_ref, out_sem, index_sem, table_sem,
):
    to_smem = pltpu.make_async_copy(index_v, index_s, index_sem)
    to_smem.start()
    to_table = pltpu.make_async_copy(table_hbm, table_ref, table_sem)
    to_table.start()

    edge_v[0] = own_ref[...]
    lane24 = iota((24, LANES), 1)
    for first, pair_at in ((0, 0), (FAR, 2)):
        west = corner_ref[pair_at, 8:32, :].astype(F32)
        east = corner_ref[pair_at + 1, 8:32, :].astype(F32)
        west2 = pltpu.roll(west, 64, 1)
        east2 = pltpu.roll(east, 64, 1)
        edge_v[0, first : first + 24, :] += jnp.where(lane24 < 64, west, east2)
        edge_v[0, first + 24 : first + 48, :] += jnp.where(lane24 < 64, west2, east)

    lane = iota((64, LANES), 1)
    for q in range(4):
        west = pltpu.roll(w_ref[...], (128 - 32 * q) % 128, 1)
        east = pltpu.roll(e_ref[...], (160 - 32 * q) % 128, 1)
        both = jnp.where(lane < 32, west, jnp.where(lane < 64, east, 0))
        edge_v[1, 32 + 64 * q : 96 + 64 * q, :] = both.astype(F32)
        for first, pair_at in ((0, 0), (288, 2)):
            west = pltpu.roll(corner_ref[pair_at, 0:8, :], (128 - 32 * q) % 128, 1)
            east = pltpu.roll(corner_ref[pair_at + 1, 0:8, :], (160 - 32 * q) % 128, 1)
            both = jnp.where(lane[0:8] < 32, west, jnp.where(lane[0:8] < 64, east, 0))
            edge_v[1, first + 8 * q : first + 8 * q + 8, :] = both.astype(F32)

    last = interleaved(edge_v, 2)
    high, low = limbs(last[:, 0:LANES])
    spread = spread_counts[256:384, :]
    minus = dot(jnp.concatenate([high, low], axis=1), jnp.concatenate([spread, spread], axis=0))
    wide = dot(last[:, LANES:].astype(BF16), spread_codes[256:384, :])

    to_table.wait()
    lane8 = iota((8, LANES), 1)
    table = []
    for k in range(2):
        pair = jnp.concatenate([table_ref[2 * k : 2 * k + 1, :], table_ref[2 * k + 1 : 2 * k + 2, :]], axis=1)
        table.append(jnp.broadcast_to(pair, (8, LANES)))
    shift = (lane8 >> 6) * CODES
    for i in range(ROWS):
        for j in range(COLS):
            block = slice(8 * i, 8 * i + 8), slice(LANES * j, LANES * (j + 1))
            code = (wide[block] + code_ref[block]).astype(I32)
            at = code + shift
            less = minus[block] + minus_ref[block]
            decay_v[pl.ds((i * COLS + j) * 8, 8), :] = jnp.where(code < CODES - TERMINAL, GAMMA, 0.0)
            for p in range(2):
                reward = jnp.take_along_axis(table[p], at, axis=1) + less
                reward_v[pl.ds((i * BOTH + p * COLS + j) * 8, 8), :] = reward
                val_a[pl.ds(((i + 1) * BOTH + p * COLS + j) * 8, 8), :] = reward

    def take(ref, i):
        return [ref[pl.ds((i * BOTH + j) * 8, 8), :] for j in range(BOTH)]

    def put(ref, i, vregs):
        for j in range(BOTH):
            ref[pl.ds((i * BOTH + j) * 8, 8), :] = vregs[j]

    def wrap(ref):
        put(ref, 0, [pltpu.roll(x, 1, 0) for x in take(ref, ROWS)])
        put(ref, ROWS + 1, [pltpu.roll(x, 7, 0) for x in take(ref, 1)])

    def ends(row):
        first = [pltpu.roll(row[p], LANES - 1, 1) for p in (0, COLS)]
        last = [pltpu.roll(row[p + COLS - 1], 1, 1) for p in (0, COLS)]
        return first, last

    def pair(above, now, first):
        right = now[1:COLS] + [first[0]] + now[COLS + 1 :] + [first[1]]
        return [jnp.maximum(a, b) for a, b in zip(above, right)]

    def sweep(source, target):
        now = take(source, 1)
        first, last = ends(now)
        here = pair(take(source, 0), now, first)
        for i in range(ROWS):
            below = take(source, i + 2)
            first, next_last = ends(below)
            under = pair(now, below, first)
            new = [None] * BOTH
            for j in range(COLS):
                decay = decay_v[pl.ds((i * COLS + j) * 8, 8), :]
                for k, p in enumerate((0, COLS)):
                    other = under[p + j - 1] if j else jnp.maximum(last[k], below[p])
                    reward = reward_v[pl.ds((i * BOTH + p + j) * 8, 8), :]
                    new[p + j] = reward + decay * jnp.maximum(here[p + j], other)
            put(target, i + 1, new)
            now, here, last = below, under, next_last
        wrap(target)

    wrap(val_a)

    def two_sweeps(index, carry):
        sweep(val_a, val_b)
        sweep(val_b, val_a)
        return carry

    lax.fori_loop(0, SWEEPS // 2, two_sweeps, 0)

    to_smem.wait()
    for k in range(16):
        for a in range(LANES):
            picked_v[pl.ds(k * LANES + a, 1), :] = val_a[pl.ds(index_s[k, a], 1), :]

    back = back_ref[...]
    stores = []
    for p in range(2):
        parts = []
        for j in range(COLS):
            rows = [val_a[pl.ds(((i + 1) * BOTH + p * COLS + j) * 8, 8), :] for i in range(ROWS)]
            parts.append(jnp.concatenate(rows, axis=0))
        block = jnp.concatenate(parts, axis=1)
        upper = block.astype(BF16)
        lower = (block - upper.astype(F32)).astype(BF16)
        flat = dot(upper, back) + dot(lower, back)
        for c in range(4):
            for i in range(ROWS):
                piece = flat[8 * i : 8 * i + 8, c * LANES : (c + 1) * LANES]
                natural_v[4 * p + c, pl.ds(i, 8, stride=ROWS), :] = piece
            stores.append(
                pltpu.make_async_copy(
                    natural_v.at[4 * p + c, pl.ds(HALO, TILE)],
                    values_out.at[2 * p + c // 2, :, pl.ds(c % 2 * LANES, LANES)],
                    out_sem.at[4 * p + c],
                )
            )
            stores[-1].start()

    diagonal = iota((LANES, LANES), 0) == iota((LANES, LANES), 1)
    for k in range(16):
        part = slice(k * LANES, (k + 1) * LANES)
        found = jnp.concatenate(
            [
                jnp.take_along_axis(
                    picked_v[k * LANES + 8 * a : k * LANES + 8 * a + 8, :],
                    select_ref[k * LANES + 8 * a : k * LANES + 8 * a + 8, :],
                    axis=1,
                )
                for a in range(16)
            ],
            axis=0,
        )
        agent_out[:, part] = jnp.sum(jnp.where(diagonal, found, 0.0), axis=0, keepdims=True)
    for store in stores:
        store.wait()


def frame(*arrays):
    return pl.pallas_call(
        frame_kernel,
        out_shape=(
            jax.ShapeDtypeStruct((4, TILE, TILE), F32),
            jax.ShapeDtypeStruct((1, AGENTS), F32),
        ),
        in_specs=[pl.BlockSpec(memory_space=pltpu.VMEM)] * 11 + [pl.BlockSpec(memory_space=pltpu.HBM)],
        out_specs=[pl.BlockSpec(memory_space=pltpu.HBM), pl.BlockSpec(memory_space=pltpu.VMEM)],
        scratch_shapes=[
            pltpu.VMEM((2, EXT, LANES), F32),
            pltpu.VMEM((ROWS * BOTH * 8, LANES), F32),
            pltpu.VMEM((ROWS * COLS * 8, LANES), F32),
            pltpu.VMEM(((ROWS + 2) * BOTH * 8, LANES), F32),
            pltpu.VMEM(((ROWS + 2) * BOTH * 8, LANES), F32),
            pltpu.VMEM((8, EXT, LANES), F32),
            pltpu.VMEM((AGENTS, LANES), F32),
            pltpu.SMEM((16, LANES), I32),
            pltpu.VMEM((4, CODES), F32),
            pltpu.SemaphoreType.DMA((8,)),
            pltpu.SemaphoreType.DMA,
            pltpu.SemaphoreType.DMA,
        ],
        compiler_params=pltpu.CompilerParams(vmem_limit_bytes=40 << 20),
        name="frame",
    )(*arrays)


def on_device(map_codes, reward_table, start_cell, agent_task, actions):
    arrived = exchange(
        map_codes, start_cell.reshape(1, AGENTS), actions, agent_task.reshape(1, AGENTS)
    )
    values, agent_value = frame(*arrived, pltpu.with_memory_space_constraint(reward_table, pltpu.HBM))
    return values, agent_value.reshape(AGENTS)


def solution(mesh):
    placed = (P("gy", "gx"), P(), P(("gx", "gy")), P(("gx", "gy")), P(None, ("gx", "gy")))
    return jax.shard_map(
        on_device,
        mesh=mesh,
        in_specs=placed,
        out_specs=(P(None, "gy", "gx"), P(("gx", "gy"))),
        check_vma=False,
    )
```

```python
import functools

import jax
import jax.numpy as jnp
from jax import lax
from jax.experimental import pallas as pl
from jax.experimental.pallas import tpu as pltpu
from jax.sharding import PartitionSpec as P

SWEEPS = 16
CODES = 64
TERMINAL = 2
GAMMA = 0.95
PENALTY = 0.5
CORNERS = ((-1, -1), (-1, 1), (1, -1), (1, 1))
SIDES = ((-1, 0), (0, -1), (0, 1), (1, 0))
NEIGHBOURS = ((-1, -1), (-1, 0), (-1, 1), (0, -1), (0, 1), (1, -1), (1, 0), (1, 1))

TILE = 256
HALO = 32
EXT = TILE + 2 * HALO
ROWS = EXT // 8
COLS = 5
LANES = 128
TASK_LANES = 64
WIDE = COLS * LANES
BOTH = 2 * COLS
AGENTS = 2048
STRIDE = 512
EDGE = 48
FAR = EXT - EDGE

F32 = jnp.float32
BF16 = jnp.bfloat16
F8 = jnp.float8_e4m3fn
I32 = jnp.int32
MESH = pl.DeviceIdType.MESH
NT = (((1,), (1,)), ((), ()))
NN = (((1,), (0,)), ((), ()))


def dot(a, b, dims=NN):
    return lax.dot_general(a, b, dims, preferred_element_type=F32)


def iota(shape, dim):
    return lax.broadcasted_iota(I32, shape, dim)


def one(match, kind):
    return jnp.where(match, 1.0, 0.0).astype(kind)


def hot(values, count):
    return one(iota((count, values.shape[1]), 0) == values, F8)


def slots(cols, low, high):
    near = (cols >= low) & (cols < low + EDGE)
    far = (cols >= high) & (cols < high + EDGE)
    return jnp.where(near, cols - low, jnp.where(far, cols - high + 64, -1))


def inner_slots(cols):
    return jnp.where((cols >= EDGE) & (cols < FAR), cols - EDGE, -1)


def interleaved(ref, tiles):
    parts = []
    for c in range(tiles):
        rows = [ref[c, pl.ds(i, 8, stride=ROWS), :] for i in range(ROWS)]
        parts.append(jnp.concatenate(rows, axis=0))
    return jnp.concatenate(parts, axis=1)


def limbs(counts):
    high = jnp.floor(counts * (1.0 / 128.0))
    low = counts - high * 128.0
    return (high * (-128.0 * PENALTY)).astype(BF16), (low * -PENALTY).astype(BF16)


def exchange_kernel(
    start_hbm, act_hbm, codes_hbm, task_hbm,
    w_out, e_out, corner_out, edge_out, code_out, minus_out,
    spread_codes, spread_counts, back_out, index_out, select_out,
    lists_v, n_v, s_v, codes_v, count_v, wide_v, start_v, act_v, task_v, cells_v, w_send, e_send, corner_send, local_sem, send_sem, recv_sem,
):
    gx = lax.axis_index("gx")
    gy = lax.axis_index("gy")

    def device(step):
        return (lax.rem(gx + step[1] + 16, 16), lax.rem(gy + step[0] + 16, 16))

    loads = [
        pltpu.make_async_copy(act_hbm, act_v, local_sem.at[0]),
        pltpu.make_async_copy(start_hbm, start_v, local_sem.at[1]),
        pltpu.make_async_copy(codes_hbm, codes_v, local_sem.at[2]),
        pltpu.make_async_copy(task_hbm, task_v, local_sem.at[3]),
    ]
    for load in loads:
        load.start()
    barrier = pltpu.get_barrier_semaphore()
    for step in NEIGHBOURS:
        pl.semaphore_signal(barrier, inc=1, device_id=device(step), device_id_type=MESH)

    slot = iota((384, LANES), 0)
    code_col = jnp.where(slot < 256, slot + HALO, jnp.where(slot < 288, slot - 256, slot))
    code_col = jnp.where(slot < 320, code_col, -1)
    count_col = jnp.where(slot < FAR - EDGE, slot + EDGE, -1)
    count_col = jnp.where((slot >= 256) & (slot < 256 + EDGE), slot - 256, count_col)
    count_col = jnp.where((slot >= 320) & (slot < 320 + EDGE), slot - 320 + FAR, count_col)
    first_col = (iota((1, LANES), 1) & 63) * COLS
    in_lane = iota((LANES, LANES), 0)
    to_lane = iota((LANES, LANES), 1)
    for j in range(COLS):
        part = slice(j * LANES, (j + 1) * LANES)
        spread_codes[:, part] = one(code_col == first_col + j, BF16)
        spread_counts[:, part] = one(count_col == first_col + j, BF16)
        column = (in_lane & 63) * COLS + (j - HALO)
        column = jnp.where((column >= 0) & (column < TILE), column + (in_lane >> 6) * TILE, -1)
        for k in range(4):
            back_out[part, k * LANES : (k + 1) * LANES] = one(column == to_lane + k * LANES, BF16)

    loads[0].wait()
    loads[1].wait()
    act = act_v[...]
    start = start_v[...]
    row = (start >> 8) + HALO
    col = (start & 255) + HALO
    row += jnp.sum((act == 2).astype(I32) - (act == 1).astype(I32), axis=0, keepdims=True)
    col += jnp.sum((act == 4).astype(I32) - (act == 3).astype(I32), axis=0, keepdims=True)
    cells_v[...] = row * STRIDE + col

    targets = [hot(inner_slots(col), 256), hot(slots(col, 0, FAR), 128), hot(slots(col, 16, 256), 128)]
    own = dot(hot(row, EXT), jnp.concatenate(targets, axis=0), NT)
    for c in range(2):
        count_v[c] = own[:, c * LANES : (c + 1) * LANES]
    edge_out[...] = own[:, 256:384]

    loads[2].wait()
    lane = iota((64, LANES), 1)
    west = jnp.zeros((64, LANES), I32)
    east = jnp.zeros((64, LANES), I32)
    for q in range(4):
        mine = (lane >= 32 * q) & (lane < 32 * q + 32)
        rows = pl.ds(64 * q, 64)
        west = jnp.where(mine, pltpu.roll(codes_v[rows, 0:128], 32 * q, 1), west)
        east = jnp.where(mine, pltpu.roll(codes_v[rows, 128:256], (32 * q + 32) % 128, 1), east)
    w_send[...] = west
    e_send[...] = east
    lane8 = iota((8, LANES), 1)
    lane24 = iota((24, LANES), 1)
    for k, (r, c) in enumerate(CORNERS):
        piece = jnp.zeros((8, LANES), I32)
        for q in range(4):
            mine = (lane8 >= 32 * q) & (lane8 < 32 * q + 32)
            rows = pl.ds((0 if r < 0 else 224) + 8 * q, 8)
            if c < 0:
                part = pltpu.roll(codes_v[rows, 0:128], 32 * q, 1)
            else:
                part = pltpu.roll(codes_v[rows, 128:256], (32 * q + 32) % 128, 1)
            piece = jnp.where(mine, part, piece)
        corner_send[k, 0:8, :] = piece
        first = 16 if r < 0 else 256
        upper = own[first : first + 24, 384:512]
        lower = own[first + 24 : first + 48, 384:512]
        if c < 0:
            lower = pltpu.roll(lower, 64, 1)
        else:
            upper = pltpu.roll(upper, 64, 1)
        corner_send[k, 8:32, :] = jnp.where(lane24 < 64, upper, lower).astype(I32)

    pl.semaphore_wait(barrier, 8)
    copies = []

    def send(source, target, step):
        k = len(copies)
        copy = pltpu.make_async_remote_copy(
            source, target, send_sem.at[k], recv_sem.at[k],
            device_id=device(step), device_id_type=MESH,
        )
        copy.start()
        copies.append(copy)

    send(cells_v, lists_v.at[1], (-1, 0))
    send(cells_v, lists_v.at[0], (1, 0))
    send(codes_v.at[pl.ds(0, 32)], s_v, (-1, 0))
    send(codes_v.at[pl.ds(224, 32)], n_v, (1, 0))
    send(cells_v, lists_v.at[3], (0, -1))
    send(cells_v, lists_v.at[2], (0, 1))
    for k, step in enumerate(CORNERS):
        send(corner_send.at[k], corner_out.at[3 - k], step)
    send(w_send, e_out, (0, -1))
    send(e_send, w_out, (0, 1))

    loads[3].wait()
    block = (row * 1639) >> 16
    group = (col * 13108) >> 16
    task = task_v[...]
    place = (row - block * ROWS + 1) * BOTH + (task >> 1) * COLS + (col - group * COLS)
    place = place * 8 + block
    lane_of = (task & 1) * TASK_LANES + group
    for k in range(16):
        part = slice(k * LANES, (k + 1) * LANES)
        index_out[k : k + 1, :] = place[:, part]
        select_out[part, :] = jnp.broadcast_to(lane_of[:, part], (LANES, LANES)).T

    for copy in copies[0:2] + copies[2:4]:
        copy.wait_recv()
    for k, first, step in ((0, 0, -1), (1, FAR, 1)):
        cells = lists_v[k]
        row = (cells >> 9) + step * TILE
        col = cells & (STRIDE - 1)
        targets = [hot(inner_slots(col), 256), hot(slots(col, 0, FAR), 128)]
        part = dot(hot(row - first, EDGE), jnp.concatenate(targets, axis=0), NT)
        band = slice(first, first + EDGE)
        for c in range(2):
            count_v[c, band, :] += part[:, c * LANES : (c + 1) * LANES]
        edge_out[band, :] += part[:, 256:384]
    for c in range(2):
        part = slice(c * LANES, (c + 1) * LANES)
        wide_v[c, 0:32, :] = n_v[:, part].astype(F32)
        wide_v[c, 32:288, :] = codes_v[:, part].astype(F32)
        wide_v[c, 288:320, :] = s_v[:, part].astype(F32)
    high, low = limbs(interleaved(count_v, 2))
    minus_out[...] = dot(high, spread_counts[0:256, :]) + dot(low, spread_counts[0:256, :])
    code_out[...] = dot(interleaved(wide_v, 2).astype(BF16), spread_codes[0:256, :])
    for k, step in ((0, 1), (1, -1)):
        copies[4 + k].wait_recv()
        cells = lists_v[3 - k]
        col = (cells & (STRIDE - 1)) + step * TILE
        edge_out[...] += dot(hot(cells >> 9, EXT), hot(slots(col, 0, FAR), 128), NT)
    for copy in copies[6:10] + copies[10:12]:
        copy.wait_recv()
    for copy in copies:
        copy.wait_send()


def exchange(codes, start, actions, task):
    return pl.pallas_call(
        exchange_kernel,
        out_shape=(
            pltpu.VMEM((64, LANES), I32),
            pltpu.VMEM((64, LANES), I32),
            pltpu.VMEM((4, 32, LANES), I32),
            pltpu.VMEM((EXT, LANES), F32),
            pltpu.VMEM((EXT, WIDE), F32),
            pltpu.VMEM((EXT, WIDE), F32),
            pltpu.VMEM((384, WIDE), BF16),
            pltpu.VMEM((384, WIDE), BF16),
            pltpu.VMEM((WIDE, 2 * TILE), BF16),
            pltpu.VMEM((16, LANES), I32),
            pltpu.VMEM((AGENTS, LANES), I32),
        ),
        in_specs=[pl.BlockSpec(memory_space=pltpu.HBM)] * 4,
        out_specs=[pl.BlockSpec(memory_space=pltpu.VMEM)] * 11,
        scratch_shapes=[
            pltpu.VMEM((4, 1, AGENTS), I32),
            pltpu.VMEM((32, TILE), I32),
            pltpu.VMEM((32, TILE), I32),
            pltpu.VMEM((TILE, TILE), I32),
            pltpu.VMEM((2, EXT, LANES), F32),
            pltpu.VMEM((2, EXT, LANES), F32),
            pltpu.VMEM((1, AGENTS), I32),
            pltpu.VMEM((16, AGENTS), I32),
            pltpu.VMEM((1, AGENTS), I32),
            pltpu.VMEM((1, AGENTS), I32),
            pltpu.VMEM((64, LANES), I32),
            pltpu.VMEM((64, LANES), I32),
            pltpu.VMEM((4, 32, LANES), I32),
            pltpu.SemaphoreType.DMA((4,)),
            pltpu.SemaphoreType.DMA((12,)),
            pltpu.SemaphoreType.DMA((12,)),
        ],
        compiler_params=pltpu.CompilerParams(
            collective_id=0, has_side_effects=True, vmem_limit_bytes=24 << 20
        ),
        name="exchange",
    )(*[pltpu.with_memory_space_constraint(x, pltpu.HBM) for x in (start, actions, codes, task)])


def frame_kernel(
    w_ref, e_ref, corner_ref, own_ref, code_ref, minus_ref,
    spread_codes, spread_counts, back_ref, index_v, select_ref, table_hbm,
    values_out, agent_out,
    edge_v, reward_v, decay_v, val_a, val_b, natural_v, picked_v,
    index_s, table_ref, out_sem, index_sem, table_sem,
):
    to_smem = pltpu.make_async_copy(index_v, index_s, index_sem)
    to_smem.start()
    to_table = pltpu.make_async_copy(table_hbm, table_ref, table_sem)
    to_table.start()

    edge_v[0] = own_ref[...]
    lane24 = iota((24, LANES), 1)
    for first, pair_at in ((0, 0), (FAR, 2)):
        west = corner_ref[pair_at, 8:32, :].astype(F32)
        east = corner_ref[pair_at + 1, 8:32, :].astype(F32)
        west2 = pltpu.roll(west, 64, 1)
        east2 = pltpu.roll(east, 64, 1)
        edge_v[0, first : first + 24, :] += jnp.where(lane24 < 64, west, east2)
        edge_v[0, first + 24 : first + 48, :] += jnp.where(lane24 < 64, west2, east)

    lane = iota((64, LANES), 1)
    for q in range(4):
        west = pltpu.roll(w_ref[...], (128 - 32 * q) % 128, 1)
        east = pltpu.roll(e_ref[...], (160 - 32 * q) % 128, 1)
        both = jnp.where(lane < 32, west, jnp.where(lane < 64, east, 0))
        edge_v[1, 32 + 64 * q : 96 + 64 * q, :] = both.astype(F32)
        for first, pair_at in ((0, 0), (288, 2)):
            west = pltpu.roll(corner_ref[pair_at, 0:8, :], (128 - 32 * q) % 128, 1)
            east = pltpu.roll(corner_ref[pair_at + 1, 0:8, :], (160 - 32 * q) % 128, 1)
            both = jnp.where(lane[0:8] < 32, west, jnp.where(lane[0:8] < 64, east, 0))
            edge_v[1, first + 8 * q : first + 8 * q + 8, :] = both.astype(F32)

    last = interleaved(edge_v, 2)
    high, low = limbs(last[:, 0:LANES])
    spread = spread_counts[256:384, :]
    minus = dot(jnp.concatenate([high, low], axis=1), jnp.concatenate([spread, spread], axis=0))
    wide = dot(last[:, LANES:].astype(BF16), spread_codes[256:384, :])

    to_table.wait()
    lane8 = iota((8, LANES), 1)
    table = []
    for k in range(2):
        pair = jnp.concatenate([table_ref[2 * k : 2 * k + 1, :], table_ref[2 * k + 1 : 2 * k + 2, :]], axis=1)
        table.append(jnp.broadcast_to(pair, (8, LANES)))
    shift = (lane8 >> 6) * CODES
    for i in range(ROWS):
        for j in range(COLS):
            block = slice(8 * i, 8 * i + 8), slice(LANES * j, LANES * (j + 1))
            code = (wide[block] + code_ref[block]).astype(I32)
            at = code + shift
            less = minus[block] + minus_ref[block]
            decay_v[pl.ds((i * COLS + j) * 8, 8), :] = jnp.where(code < CODES - TERMINAL, GAMMA, 0.0)
            for p in range(2):
                reward = jnp.take_along_axis(table[p], at, axis=1) + less
                reward_v[pl.ds((i * BOTH + p * COLS + j) * 8, 8), :] = reward
                val_a[pl.ds(((i + 1) * BOTH + p * COLS + j) * 8, 8), :] = reward

    def take(ref, i):
        return [ref[pl.ds((i * BOTH + j) * 8, 8), :] for j in range(BOTH)]

    def put(ref, i, vregs):
        for j in range(BOTH):
            ref[pl.ds((i * BOTH + j) * 8, 8), :] = vregs[j]

    def wrap(ref):
        put(ref, 0, [pltpu.roll(x, 1, 0) for x in take(ref, ROWS)])
        put(ref, ROWS + 1, [pltpu.roll(x, 7, 0) for x in take(ref, 1)])

    def ends(row):
        first = [pltpu.roll(row[p], LANES - 1, 1) for p in (0, COLS)]
        last = [pltpu.roll(row[p + COLS - 1], 1, 1) for p in (0, COLS)]
        return first, last

    def pair(above, now, first):
        right = now[1:COLS] + [first[0]] + now[COLS + 1 :] + [first[1]]
        return [jnp.maximum(a, b) for a, b in zip(above, right)]

    def sweep(source, target):
        now = take(source, 1)
        first, last = ends(now)
        here = pair(take(source, 0), now, first)
        for i in range(ROWS):
            below = take(source, i + 2)
            first, next_last = ends(below)
            under = pair(now, below, first)
            new = [None] * BOTH
            for j in range(COLS):
                decay = decay_v[pl.ds((i * COLS + j) * 8, 8), :]
                for k, p in enumerate((0, COLS)):
                    other = under[p + j - 1] if j else jnp.maximum(last[k], below[p])
                    reward = reward_v[pl.ds((i * BOTH + p + j) * 8, 8), :]
                    new[p + j] = reward + decay * jnp.maximum(here[p + j], other)
            put(target, i + 1, new)
            now, here, last = below, under, next_last
        wrap(target)

    wrap(val_a)

    def two_sweeps(index, carry):
        sweep(val_a, val_b)
        sweep(val_b, val_a)
        return carry

    lax.fori_loop(0, SWEEPS // 2 - 1, two_sweeps, 0)
    two_sweeps(0, 0)

    to_smem.wait()
    for k in range(16):
        for a in range(LANES):
            picked_v[pl.ds(k * LANES + a, 1), :] = val_a[pl.ds(index_s[k, a], 1), :]

    back = back_ref[...]
    stores = []
    for p in range(2):
        parts = []
        for j in range(COLS):
            rows = [val_a[pl.ds(((i + 1) * BOTH + p * COLS + j) * 8, 8), :] for i in range(ROWS)]
            parts.append(jnp.concatenate(rows, axis=0))
        block = jnp.concatenate(parts, axis=1)
        upper = block.astype(BF16)
        lower = (block - upper.astype(F32)).astype(BF16)
        flat = dot(upper, back) + dot(lower, back)
        for c in range(4):
            for i in range(ROWS):
                piece = flat[8 * i : 8 * i + 8, c * LANES : (c + 1) * LANES]
                natural_v[4 * p + c, pl.ds(i, 8, stride=ROWS), :] = piece
            stores.append(
                pltpu.make_async_copy(
                    natural_v.at[4 * p + c, pl.ds(HALO, TILE)],
                    values_out.at[2 * p + c // 2, :, pl.ds(c % 2 * LANES, LANES)],
                    out_sem.at[4 * p + c],
                )
            )
            stores[-1].start()

    diagonal = iota((LANES, LANES), 0) == iota((LANES, LANES), 1)
    for k in range(16):
        part = slice(k * LANES, (k + 1) * LANES)
        found = jnp.concatenate(
            [
                jnp.take_along_axis(
                    picked_v[k * LANES + 8 * a : k * LANES + 8 * a + 8, :],
                    select_ref[k * LANES + 8 * a : k * LANES + 8 * a + 8, :],
                    axis=1,
                )
                for a in range(16)
            ],
            axis=0,
        )
        agent_out[:, part] = jnp.sum(jnp.where(diagonal, found, 0.0), axis=0, keepdims=True)
    for store in stores:
        store.wait()


def frame(*arrays):
    return pl.pallas_call(
        frame_kernel,
        out_shape=(
            jax.ShapeDtypeStruct((4, TILE, TILE), F32),
            jax.ShapeDtypeStruct((1, AGENTS), F32),
        ),
        in_specs=[pl.BlockSpec(memory_space=pltpu.VMEM)] * 11 + [pl.BlockSpec(memory_space=pltpu.HBM)],
        out_specs=[pl.BlockSpec(memory_space=pltpu.HBM), pl.BlockSpec(memory_space=pltpu.VMEM)],
        scratch_shapes=[
            pltpu.VMEM((2, EXT, LANES), F32),
            pltpu.VMEM((ROWS * BOTH * 8, LANES), F32),
            pltpu.VMEM((ROWS * COLS * 8, LANES), F32),
            pltpu.VMEM(((ROWS + 2) * BOTH * 8, LANES), F32),
            pltpu.VMEM(((ROWS + 2) * BOTH * 8, LANES), F32),
            pltpu.VMEM((8, EXT, LANES), F32),
            pltpu.VMEM((AGENTS, LANES), F32),
            pltpu.SMEM((16, LANES), I32),
            pltpu.VMEM((4, CODES), F32),
            pltpu.SemaphoreType.DMA((8,)),
            pltpu.SemaphoreType.DMA,
            pltpu.SemaphoreType.DMA,
        ],
        compiler_params=pltpu.CompilerParams(vmem_limit_bytes=40 << 20),
        name="frame",
    )(*arrays)


def on_device(map_codes, reward_table, start_cell, agent_task, actions):
    arrived = exchange(
        map_codes, start_cell.reshape(1, AGENTS), actions, agent_task.reshape(1, AGENTS)
    )
    values, agent_value = frame(*arrived, pltpu.with_memory_space_constraint(reward_table, pltpu.HBM))
    return values, agent_value.reshape(AGENTS)


def solution(mesh):
    placed = (P("gy", "gx"), P(), P(("gx", "gy")), P(("gx", "gy")), P(None, ("gx", "gy")))
    return jax.shard_map(
        on_device,
        mesh=mesh,
        in_specs=placed,
        out_specs=(P(None, "gy", "gx"), P(("gx", "gy"))),
        check_vma=False,
    )
```

```python
import functools

import jax
import jax.numpy as jnp
from jax import lax
from jax.experimental import pallas as pl
from jax.experimental.pallas import tpu as pltpu
from jax.sharding import PartitionSpec as P

SWEEPS = 16
CODES = 64
TERMINAL = 2
GAMMA = 0.95
PENALTY = 0.5
CORNERS = ((-1, -1), (-1, 1), (1, -1), (1, 1))
SIDES = ((-1, 0), (0, -1), (0, 1), (1, 0))
NEIGHBOURS = ((-1, -1), (-1, 0), (-1, 1), (0, -1), (0, 1), (1, -1), (1, 0), (1, 1))

TILE = 256
HALO = 32
EXT = TILE + 2 * HALO
ROWS = EXT // 8
COLS = 5
LANES = 128
TASK_LANES = 64
WIDE = COLS * LANES
BOTH = 2 * COLS
AGENTS = 2048
STRIDE = 512
EDGE = 48
FAR = EXT - EDGE

F32 = jnp.float32
BF16 = jnp.bfloat16
F8 = jnp.float8_e4m3fn
I32 = jnp.int32
MESH = pl.DeviceIdType.MESH
NT = (((1,), (1,)), ((), ()))
NN = (((1,), (0,)), ((), ()))


def dot(a, b, dims=NN):
    return lax.dot_general(a, b, dims, preferred_element_type=F32)


def iota(shape, dim):
    return lax.broadcasted_iota(I32, shape, dim)


def one(match, kind):
    return jnp.where(match, 1.0, 0.0).astype(kind)


def hot(values, count):
    return one(iota((count, values.shape[1]), 0) == values, F8)


def slots(cols, low, high):
    near = (cols >= low) & (cols < low + EDGE)
    far = (cols >= high) & (cols < high + EDGE)
    return jnp.where(near, cols - low, jnp.where(far, cols - high + 64, -1))


def inner_slots(cols):
    return jnp.where((cols >= EDGE) & (cols < FAR), cols - EDGE, -1)


def interleaved(ref, tiles):
    parts = []
    for c in range(tiles):
        rows = [ref[c, pl.ds(i, 8, stride=ROWS), :] for i in range(ROWS)]
        parts.append(jnp.concatenate(rows, axis=0))
    return jnp.concatenate(parts, axis=1)


def limbs(counts):
    high = jnp.floor(counts * (1.0 / 128.0))
    low = counts - high * 128.0
    return (high * (-128.0 * PENALTY)).astype(BF16), (low * -PENALTY).astype(BF16)


def exchange_kernel(
    start_hbm, act_hbm, codes_hbm, task_hbm,
    w_out, e_out, corner_out, edge_out, code_out, minus_out,
    spread_codes, spread_counts, back_out, index_out, select_out,
    lists_v, n_v, s_v, codes_v, count_v, wide_v, start_v, act_v, task_v, cells_v, w_send, e_send, corner_send, local_sem, send_sem, recv_sem,
):
    gx = lax.axis_index("gx")
    gy = lax.axis_index("gy")

    def device(step):
        return (lax.rem(gx + step[1] + 16, 16), lax.rem(gy + step[0] + 16, 16))

    loads = [
        pltpu.make_async_copy(act_hbm, act_v, local_sem.at[0]),
        pltpu.make_async_copy(start_hbm, start_v, local_sem.at[1]),
        pltpu.make_async_copy(codes_hbm, codes_v, local_sem.at[2]),
        pltpu.make_async_copy(task_hbm, task_v, local_sem.at[3]),
    ]
    for load in loads:
        load.start()
    barrier = pltpu.get_barrier_semaphore()
    for step in NEIGHBOURS:
        pl.semaphore_signal(barrier, inc=1, device_id=device(step), device_id_type=MESH)

    slot = iota((384, LANES), 0)
    code_col = jnp.where(slot < 256, slot + HALO, jnp.where(slot < 288, slot - 256, slot))
    code_col = jnp.where(slot < 320, code_col, -1)
    count_col = jnp.where(slot < FAR - EDGE, slot + EDGE, -1)
    count_col = jnp.where((slot >= 256) & (slot < 256 + EDGE), slot - 256, count_col)
    count_col = jnp.where((slot >= 320) & (slot < 320 + EDGE), slot - 320 + FAR, count_col)
    first_col = (iota((1, LANES), 1) & 63) * COLS
    in_lane = iota((LANES, LANES), 0)
    to_lane = iota((LANES, LANES), 1)
    for j in range(COLS):
        part = slice(j * LANES, (j + 1) * LANES)
        spread_codes[:, part] = one(code_col == first_col + j, BF16)
        spread_counts[:, part] = one(count_col == first_col + j, BF16)
        column = (in_lane & 63) * COLS + (j - HALO)
        column = jnp.where((column >= 0) & (column < TILE), column + (in_lane >> 6) * TILE, -1)
        for k in range(4):
            back_out[part, k * LANES : (k + 1) * LANES] = one(column == to_lane + k * LANES, BF16)

    loads[0].wait()
    loads[1].wait()
    act = act_v[...]
    start = start_v[...]
    row = (start >> 8) + HALO
    col = (start & 255) + HALO
    row += jnp.sum((act == 2).astype(I32) - (act == 1).astype(I32), axis=0, keepdims=True)
    col += jnp.sum((act == 4).astype(I32) - (act == 3).astype(I32), axis=0, keepdims=True)
    cells_v[...] = row * STRIDE + col

    loads[2].wait()
    lane = iota((64, LANES), 1)
    west = jnp.zeros((64, LANES), I32)
    east = jnp.zeros((64, LANES), I32)
    for q in range(4):
        mine = (lane >= 32 * q) & (lane < 32 * q + 32)
        rows = pl.ds(64 * q, 64)
        west = jnp.where(mine, pltpu.roll(codes_v[rows, 0:128], 32 * q, 1), west)
        east = jnp.where(mine, pltpu.roll(codes_v[rows, 128:256], (32 * q + 32) % 128, 1), east)
    w_send[...] = west
    e_send[...] = east
    pl.semaphore_wait(barrier, 8)
    copies = []

    def send(source, target, step):
        k = len(copies)
        copy = pltpu.make_async_remote_copy(
            source, target, send_sem.at[k], recv_sem.at[k],
            device_id=device(step), device_id_type=MESH,
        )
        copy.start()
        copies.append(copy)

    send(cells_v, lists_v.at[1], (-1, 0))
    send(cells_v, lists_v.at[0], (1, 0))
    send(codes_v.at[pl.ds(0, 32)], s_v, (-1, 0))
    send(codes_v.at[pl.ds(224, 32)], n_v, (1, 0))
    send(cells_v, lists_v.at[3], (0, -1))
    send(cells_v, lists_v.at[2], (0, 1))
    send(w_send, e_out, (0, -1))
    send(e_send, w_out, (0, 1))

    targets = [hot(inner_slots(col), 256), hot(slots(col, 0, FAR), 128), hot(slots(col, 16, 256), 128)]
    own = dot(hot(row, EXT), jnp.concatenate(targets, axis=0), NT)
    for c in range(2):
        count_v[c] = own[:, c * LANES : (c + 1) * LANES]
    edge_out[...] = own[:, 256:384]

    lane8 = iota((8, LANES), 1)
    lane24 = iota((24, LANES), 1)
    for k, (r, c) in enumerate(CORNERS):
        piece = jnp.zeros((8, LANES), I32)
        for q in range(4):
            mine = (lane8 >= 32 * q) & (lane8 < 32 * q + 32)
            rows = pl.ds((0 if r < 0 else 224) + 8 * q, 8)
            if c < 0:
                part = pltpu.roll(codes_v[rows, 0:128], 32 * q, 1)
            else:
                part = pltpu.roll(codes_v[rows, 128:256], (32 * q + 32) % 128, 1)
            piece = jnp.where(mine, part, piece)
        corner_send[k, 0:8, :] = piece
        first = 16 if r < 0 else 256
        upper = own[first : first + 24, 384:512]
        lower = own[first + 24 : first + 48, 384:512]
        if c < 0:
            lower = pltpu.roll(lower, 64, 1)
        else:
            upper = pltpu.roll(upper, 64, 1)
        corner_send[k, 8:32, :] = jnp.where(lane24 < 64, upper, lower).astype(I32)

    for k, step in enumerate(CORNERS):
        send(corner_send.at[k], corner_out.at[3 - k], step)

    loads[3].wait()
    block = (row * 1639) >> 16
    group = (col * 13108) >> 16
    task = task_v[...]
    place = (row - block * ROWS + 1) * BOTH + (task >> 1) * COLS + (col - group * COLS)
    place = place * 8 + block
    lane_of = (task & 1) * TASK_LANES + group
    for k in range(16):
        part = slice(k * LANES, (k + 1) * LANES)
        index_out[k : k + 1, :] = place[:, part]
        select_out[part, :] = jnp.broadcast_to(lane_of[:, part], (LANES, LANES)).T

    for copy in copies[0:2] + copies[2:4]:
        copy.wait_recv()
    for k, first, step in ((0, 0, -1), (1, FAR, 1)):
        cells = lists_v[k]
        row = (cells >> 9) + step * TILE
        col = cells & (STRIDE - 1)
        targets = [hot(inner_slots(col), 256), hot(slots(col, 0, FAR), 128)]
        part = dot(hot(row - first, EDGE), jnp.concatenate(targets, axis=0), NT)
        band = slice(first, first + EDGE)
        for c in range(2):
            count_v[c, band, :] += part[:, c * LANES : (c + 1) * LANES]
        edge_out[band, :] += part[:, 256:384]
    for c in range(2):
        part = slice(c * LANES, (c + 1) * LANES)
        wide_v[c, 0:32, :] = n_v[:, part].astype(F32)
        wide_v[c, 32:288, :] = codes_v[:, part].astype(F32)
        wide_v[c, 288:320, :] = s_v[:, part].astype(F32)
    high, low = limbs(interleaved(count_v, 2))
    minus_out[...] = dot(high, spread_counts[0:256, :]) + dot(low, spread_counts[0:256, :])
    code_out[...] = dot(interleaved(wide_v, 2).astype(BF16), spread_codes[0:256, :])
    for k, step in ((0, 1), (1, -1)):
        copies[4 + k].wait_recv()
        cells = lists_v[3 - k]
        col = (cells & (STRIDE - 1)) + step * TILE
        edge_out[...] += dot(hot(cells >> 9, EXT), hot(slots(col, 0, FAR), 128), NT)
    for copy in copies[6:10] + copies[10:12]:
        copy.wait_recv()
    for copy in copies:
        copy.wait_send()


def exchange(codes, start, actions, task):
    return pl.pallas_call(
        exchange_kernel,
        out_shape=(
            pltpu.VMEM((64, LANES), I32),
            pltpu.VMEM((64, LANES), I32),
            pltpu.VMEM((4, 32, LANES), I32),
            pltpu.VMEM((EXT, LANES), F32),
            pltpu.VMEM((EXT, WIDE), F32),
            pltpu.VMEM((EXT, WIDE), F32),
            pltpu.VMEM((384, WIDE), BF16),
            pltpu.VMEM((384, WIDE), BF16),
            pltpu.VMEM((WIDE, 2 * TILE), BF16),
            pltpu.VMEM((16, LANES), I32),
            pltpu.VMEM((AGENTS, LANES), I32),
        ),
        in_specs=[pl.BlockSpec(memory_space=pltpu.HBM)] * 4,
        out_specs=[pl.BlockSpec(memory_space=pltpu.VMEM)] * 11,
        scratch_shapes=[
            pltpu.VMEM((4, 1, AGENTS), I32),
            pltpu.VMEM((32, TILE), I32),
            pltpu.VMEM((32, TILE), I32),
            pltpu.VMEM((TILE, TILE), I32),
            pltpu.VMEM((2, EXT, LANES), F32),
            pltpu.VMEM((2, EXT, LANES), F32),
            pltpu.VMEM((1, AGENTS), I32),
            pltpu.VMEM((16, AGENTS), I32),
            pltpu.VMEM((1, AGENTS), I32),
            pltpu.VMEM((1, AGENTS), I32),
            pltpu.VMEM((64, LANES), I32),
            pltpu.VMEM((64, LANES), I32),
            pltpu.VMEM((4, 32, LANES), I32),
            pltpu.SemaphoreType.DMA((4,)),
            pltpu.SemaphoreType.DMA((12,)),
            pltpu.SemaphoreType.DMA((12,)),
        ],
        compiler_params=pltpu.CompilerParams(
            collective_id=0, has_side_effects=True, vmem_limit_bytes=24 << 20
        ),
        name="exchange",
    )(*[pltpu.with_memory_space_constraint(x, pltpu.HBM) for x in (start, actions, codes, task)])


def frame_kernel(
    w_ref, e_ref, corner_ref, own_ref, code_ref, minus_ref,
    spread_codes, spread_counts, back_ref, index_v, select_ref, table_hbm,
    values_out, agent_out,
    edge_v, reward_v, decay_v, val_a, val_b, natural_v, picked_v,
    index_s, table_ref, out_sem, index_sem, table_sem,
):
    to_smem = pltpu.make_async_copy(index_v, index_s, index_sem)
    to_smem.start()
    to_table = pltpu.make_async_copy(table_hbm, table_ref, table_sem)
    to_table.start()

    edge_v[0] = own_ref[...]
    lane24 = iota((24, LANES), 1)
    for first, pair_at in ((0, 0), (FAR, 2)):
        west = corner_ref[pair_at, 8:32, :].astype(F32)
        east = corner_ref[pair_at + 1, 8:32, :].astype(F32)
        west2 = pltpu.roll(west, 64, 1)
        east2 = pltpu.roll(east, 64, 1)
        edge_v[0, first : first + 24, :] += jnp.where(lane24 < 64, west, east2)
        edge_v[0, first + 24 : first + 48, :] += jnp.where(lane24 < 64, west2, east)

    lane = iota((64, LANES), 1)
    for q in range(4):
        west = pltpu.roll(w_ref[...], (128 - 32 * q) % 128, 1)
        east = pltpu.roll(e_ref[...], (160 - 32 * q) % 128, 1)
        both = jnp.where(lane < 32, west, jnp.where(lane < 64, east, 0))
        edge_v[1, 32 + 64 * q : 96 + 64 * q, :] = both.astype(F32)
        for first, pair_at in ((0, 0), (288, 2)):
            west = pltpu.roll(corner_ref[pair_at, 0:8, :], (128 - 32 * q) % 128, 1)
            east = pltpu.roll(corner_ref[pair_at + 1, 0:8, :], (160 - 32 * q) % 128, 1)
            both = jnp.where(lane[0:8] < 32, west, jnp.where(lane[0:8] < 64, east, 0))
            edge_v[1, first + 8 * q : first + 8 * q + 8, :] = both.astype(F32)

    last = interleaved(edge_v, 2)
    high, low = limbs(last[:, 0:LANES])
    spread = spread_counts[256:384, :]
    minus = dot(jnp.concatenate([high, low], axis=1), jnp.concatenate([spread, spread], axis=0))
    wide = dot(last[:, LANES:].astype(BF16), spread_codes[256:384, :])

    to_table.wait()
    lane8 = iota((8, LANES), 1)
    table = []
    for k in range(2):
        pair = jnp.concatenate([table_ref[2 * k : 2 * k + 1, :], table_ref[2 * k + 1 : 2 * k + 2, :]], axis=1)
        table.append(jnp.broadcast_to(pair, (8, LANES)))
    shift = (lane8 >> 6) * CODES
    for i in range(ROWS):
        for j in range(COLS):
            block = slice(8 * i, 8 * i + 8), slice(LANES * j, LANES * (j + 1))
            code = (wide[block] + code_ref[block]).astype(I32)
            at = code + shift
            less = minus[block] + minus_ref[block]
            decay_v[pl.ds((i * COLS + j) * 8, 8), :] = jnp.where(code < CODES - TERMINAL, GAMMA, 0.0)
            for p in range(2):
                reward = jnp.take_along_axis(table[p], at, axis=1) + less
                reward_v[pl.ds((i * BOTH + p * COLS + j) * 8, 8), :] = reward
                val_a[pl.ds(((i + 1) * BOTH + p * COLS + j) * 8, 8), :] = reward

    def take(ref, i):
        return [ref[pl.ds((i * BOTH + j) * 8, 8), :] for j in range(BOTH)]

    def put(ref, i, vregs):
        for j in range(BOTH):
            ref[pl.ds((i * BOTH + j) * 8, 8), :] = vregs[j]

    def wrap(ref):
        put(ref, 0, [pltpu.roll(x, 1, 0) for x in take(ref, ROWS)])
        put(ref, ROWS + 1, [pltpu.roll(x, 7, 0) for x in take(ref, 1)])

    def ends(row):
        first = [pltpu.roll(row[p], LANES - 1, 1) for p in (0, COLS)]
        last = [pltpu.roll(row[p + COLS - 1], 1, 1) for p in (0, COLS)]
        return first, last

    def pair(above, now, first):
        right = now[1:COLS] + [first[0]] + now[COLS + 1 :] + [first[1]]
        return [jnp.maximum(a, b) for a, b in zip(above, right)]

    def sweep(source, target):
        now = take(source, 1)
        first, last = ends(now)
        here = pair(take(source, 0), now, first)
        for i in range(ROWS):
            below = take(source, i + 2)
            first, next_last = ends(below)
            under = pair(now, below, first)
            new = [None] * BOTH
            for j in range(COLS):
                decay = decay_v[pl.ds((i * COLS + j) * 8, 8), :]
                for k, p in enumerate((0, COLS)):
                    other = under[p + j - 1] if j else jnp.maximum(last[k], below[p])
                    reward = reward_v[pl.ds((i * BOTH + p + j) * 8, 8), :]
                    new[p + j] = reward + decay * jnp.maximum(here[p + j], other)
            put(target, i + 1, new)
            now, here, last = below, under, next_last
        wrap(target)

    wrap(val_a)

    def two_sweeps(index, carry):
        sweep(val_a, val_b)
        sweep(val_b, val_a)
        return carry

    lax.fori_loop(0, SWEEPS // 2 - 1, two_sweeps, 0)
    two_sweeps(0, 0)

    to_smem.wait()
    for k in range(16):
        for a in range(LANES):
            picked_v[pl.ds(k * LANES + a, 1), :] = val_a[pl.ds(index_s[k, a], 1), :]

    back = back_ref[...]
    stores = []
    for p in range(2):
        parts = []
        for j in range(COLS):
            rows = [val_a[pl.ds(((i + 1) * BOTH + p * COLS + j) * 8, 8), :] for i in range(ROWS)]
            parts.append(jnp.concatenate(rows, axis=0))
        block = jnp.concatenate(parts, axis=1)
        upper = block.astype(BF16)
        lower = (block - upper.astype(F32)).astype(BF16)
        flat = dot(upper, back) + dot(lower, back)
        for c in range(4):
            for i in range(ROWS):
                piece = flat[8 * i : 8 * i + 8, c * LANES : (c + 1) * LANES]
                natural_v[4 * p + c, pl.ds(i, 8, stride=ROWS), :] = piece
            stores.append(
                pltpu.make_async_copy(
                    natural_v.at[4 * p + c, pl.ds(HALO, TILE)],
                    values_out.at[2 * p + c // 2, :, pl.ds(c % 2 * LANES, LANES)],
                    out_sem.at[4 * p + c],
                )
            )
            stores[-1].start()

    diagonal = iota((LANES, LANES), 0) == iota((LANES, LANES), 1)
    for k in range(16):
        part = slice(k * LANES, (k + 1) * LANES)
        found = jnp.concatenate(
            [
                jnp.take_along_axis(
                    picked_v[k * LANES + 8 * a : k * LANES + 8 * a + 8, :],
                    select_ref[k * LANES + 8 * a : k * LANES + 8 * a + 8, :],
                    axis=1,
                )
                for a in range(16)
            ],
            axis=0,
        )
        agent_out[:, part] = jnp.sum(jnp.where(diagonal, found, 0.0), axis=0, keepdims=True)
    for store in stores:
        store.wait()


def frame(*arrays):
    return pl.pallas_call(
        frame_kernel,
        out_shape=(
            jax.ShapeDtypeStruct((4, TILE, TILE), F32),
            jax.ShapeDtypeStruct((1, AGENTS), F32),
        ),
        in_specs=[pl.BlockSpec(memory_space=pltpu.VMEM)] * 11 + [pl.BlockSpec(memory_space=pltpu.HBM)],
        out_specs=[pl.BlockSpec(memory_space=pltpu.HBM), pl.BlockSpec(memory_space=pltpu.VMEM)],
        scratch_shapes=[
            pltpu.VMEM((2, EXT, LANES), F32),
            pltpu.VMEM((ROWS * BOTH * 8, LANES), F32),
            pltpu.VMEM((ROWS * COLS * 8, LANES), F32),
            pltpu.VMEM(((ROWS + 2) * BOTH * 8, LANES), F32),
            pltpu.VMEM(((ROWS + 2) * BOTH * 8, LANES), F32),
            pltpu.VMEM((8, EXT, LANES), F32),
            pltpu.VMEM((AGENTS, LANES), F32),
            pltpu.SMEM((16, LANES), I32),
            pltpu.VMEM((4, CODES), F32),
            pltpu.SemaphoreType.DMA((8,)),
            pltpu.SemaphoreType.DMA,
            pltpu.SemaphoreType.DMA,
        ],
        compiler_params=pltpu.CompilerParams(vmem_limit_bytes=40 << 20),
        name="frame",
    )(*arrays)


def on_device(map_codes, reward_table, start_cell, agent_task, actions):
    arrived = exchange(
        map_codes, start_cell.reshape(1, AGENTS), actions, agent_task.reshape(1, AGENTS)
    )
    values, agent_value = frame(*arrived, pltpu.with_memory_space_constraint(reward_table, pltpu.HBM))
    return values, agent_value.reshape(AGENTS)


def solution(mesh):
    placed = (P("gy", "gx"), P(), P(("gx", "gy")), P(("gx", "gy")), P(None, ("gx", "gy")))
    return jax.shard_map(
        on_device,
        mesh=mesh,
        in_specs=placed,
        out_specs=(P(None, "gy", "gx"), P(("gx", "gy"))),
        check_vma=False,
    )
```
